128 devices in a mesh: gx: 8 (over y, core), gy: 4 (over x), gz: 4 (over z).
Axes of the slice: x: 4, y: 4, z: 4, core: 2. Of those that a mesh axis runs over, the one named last changes fastest.
Arguments:
- initial_warmth: float32 [512, 512, 1024], P('gx', 'gy', 'gz'), may hold values from -6 to 6
- heat_supply: float32 [512, 512, 1024], P('gx', 'gy', 'gz'), may hold values from -98304 to 98306
Outputs:
- updated: float32 [512, 512, 1024], P('gx', 'gy', 'gz')
The draws below stay inside these ranges and needn't reach their ends.
All inputs are finite; a program needn't handle non-finite values.
Results may differ from the reference program's by a relative error of at most 0.0009.
Values sent between devices are 32-bit elements; how exact they have to be, the bound alone decides.
A program may use at most 128 MiB of HBM per device.

```python
import jax
import jax.numpy as jnp
from jax import lax

MESH_COUNT_EAST = 512
MESH_COUNT_NORTH = 512
MESH_COUNT_UPWARD = 1024
RX = 65536
RY = 65536
RZ = 262144


def draw_heat_supply(key, part):
    first_key = jax.random.fold_in(key, 11)
    second_key = jax.random.fold_in(key, 12)
    base_values = jax.random.uniform(first_key, (MESH_COUNT_EAST, MESH_COUNT_NORTH, MESH_COUNT_UPWARD), jnp.float32, -1.0, 1.0)
    spread_values = jax.random.uniform(second_key, (MESH_COUNT_EAST, MESH_COUNT_NORTH, MESH_COUNT_UPWARD), jnp.float32, 0.5, 2.0)
    result = base_values * spread_values * ((RX + RY + RZ) // 8)
    return result


def levels(own_key, shape, split, low, top_value):
    def one(position, blocks):
        draws = jax.random.uniform(jax.random.fold_in(jax.random.fold_in(own_key, 6), position), (blocks,), jnp.float32, low / len(split), top_value / len(split))
        return jnp.repeat(jnp.exp(draws), shape[position] // blocks).reshape((-1,) + (1,) * (len(shape) - position - 1))

    level = one(*split[0])
    for cut in split[1:]:
        level = level * one(*cut)
    return level


def bell_draw(rng, shape, spread, limit, split=(), held_as=jnp.bfloat16):
    array = spread * jax.random.normal(rng, shape, jnp.float32)
    if split:
        array = array * levels(rng, shape, split, -0.22, 0.18)
    return jnp.clip(array, -limit, limit).astype(held_as)


def setup_inputs(seed: int = 0) -> dict:
    splits = jax.random.split(jax.random.key(seed), 3)
    return {
        "initial_warmth": bell_draw(splits[0], (MESH_COUNT_EAST, MESH_COUNT_NORTH, MESH_COUNT_UPWARD), 1.0, 6.0, ((0, 8), (1, 4), (2, 4)), jnp.float32),
        "heat_supply": draw_heat_supply(jax.random.fold_in(splits[2], 71), 0),
    }


def line_solve(values, factor, axis_pos):
    moved_axis = jnp.moveaxis(values, axis_pos, -2)
    length = moved_axis.shape[-2]
    leading = moved_axis.shape[:-2]
    diagonal = jnp.full(leading + (length,), 1.0 + factor, dtype=jnp.float32)
    sideband = jnp.full(leading + (length,), -0.5 * factor, dtype=jnp.float32)
    lower_band = sideband.at[..., 0].set(0.0)
    upper_band = sideband.at[..., length - 1].set(0.0)
    solved = lax.linalg.tridiagonal_solve(lower_band, diagonal, upper_band, moved_axis)
    return jnp.moveaxis(solved, -2, axis_pos)

def reference(initial_warmth, heat_supply):
    bordered_grid = jnp.pad(initial_warmth, 1)
    coefficient_east = RX * 1.0
    coefficient_north = RY * 1.0
    coefficient_upward = RZ * 1.0
    forward_increment = coefficient_east * (bordered_grid[2:, 1:-1, 1:-1] - 2.0 * initial_warmth + bordered_grid[:-2, 1:-1, 1:-1])
    forward_increment = forward_increment + coefficient_north * (bordered_grid[1:-1, 2:, 1:-1] - 2.0 * initial_warmth + bordered_grid[1:-1, :-2, 1:-1])
    forward_increment = forward_increment + coefficient_upward * (bordered_grid[1:-1, 1:-1, 2:] - 2.0 * initial_warmth + bordered_grid[1:-1, 1:-1, :-2])
    forward_increment = forward_increment + heat_supply
    section_one = line_solve(forward_increment, coefficient_east, 0)
    section_two = line_solve(section_one, coefficient_north, 1)
    upward_portion = line_solve(section_two, coefficient_upward, 2)
    return initial_warmth + upward_portion
```

```python
import functools

import jax
import jax.numpy as jnp
import numpy as np
from jax import lax
from jax.experimental import pallas as pl
from jax.experimental.pallas import tpu as pltpu
from jax.sharding import PartitionSpec as P

MESH = pl.DeviceIdType.MESH
HIGH = lax.Precision.HIGHEST
F32 = jnp.float32
BF16 = jnp.bfloat16
LANES = 128
SUB = 8


def generators(whole, factor):
    half = 0.5 * factor
    theta = np.arccosh(1.0 + 0.5 / half)
    scale = np.sqrt(1.0 / (half * np.sinh(theta) * np.sinh((whole + 1) * theta)))
    index = np.arange(whole, dtype=np.float64)
    return np.sinh((index + 1) * theta) * scale, np.sinh((whole - index) * theta) * scale


def diagonal_blocks(u, v, members):
    extent = u.shape[0] // members
    blocks = []
    for member in range(members):
        part = slice(member * extent, (member + 1) * extent)
        own_u, own_v = u[part], v[part]
        lower = np.outer(own_v, own_u)
        blocks.append(np.where(np.tri(extent, dtype=bool), lower, lower.T))
    return np.stack(blocks)


def split_bf16(values):
    high = values.astype(np.float32).astype(BF16)
    low = (values - high.astype(np.float64)).astype(np.float32).astype(BF16)
    return np.asarray(high), np.asarray(low)


def split(values):
    high = values.astype(BF16)
    return high, (values - high.astype(F32)).astype(BF16)


def make_tables(shape, members):
    east, north, upward = shape
    wholes = [extent * count for extent, count in zip(shape, members)]
    factors = [float(whole * whole // 4) for whole in wholes]
    order = np.arange(north)
    order = (north // SUB) * (order % SUB) + order // SUB

    ux, vx = generators(wholes[0], factors[0])
    uy, vy = generators(wholes[1], factors[1])
    uz, vz = generators(wholes[2], factors[2])
    tables = {"factors": factors}
    tables["x"] = np.stack([ux, vx]).astype(np.float32)

    own = [np.stack([w.reshape(members[1], north)[:, order] for w in (uy, vy)], 1)][0]
    tables["y"] = np.repeat(own[..., None], LANES, -1).astype(np.float32)
    by = diagonal_blocks(uy, vy, members[1])[:, order][:, :, order]
    tables["by"] = by.astype(np.float32)
    mom = np.zeros((members[1], 2, 2, north, LANES), np.float32)
    for kind in range(2):
        for m in range(2):
            mom[:, kind, m, :, m] = own[:, kind]
    tables["ymom"] = mom
    wy = np.zeros((members[1], north, LANES), np.float32)
    wy[:, :, 0] = own[:, 1]
    wy[:, :, 1] = own[:, 0]
    tables["wy"] = wy

    bz = diagonal_blocks(uz, vz, members[2])
    tables["bzh"], tables["bzl"] = split_bf16(bz)
    zu, zv = uz.reshape(members[2], upward), vz.reshape(members[2], upward)
    uh, ul = split_bf16(zu)
    vh, vl = split_bf16(zv)
    zero = np.zeros_like(uh)
    tables["zmom"] = np.stack([uh, ul, vh, vl] + [zero] * 12, 1)
    tables["zadd"] = np.stack([vh, vh, vl, uh, uh, ul, zero, zero], 1)
    wz = np.zeros((members[2], LANES, upward), np.float32)
    wz[:, 0] = zv
    wz[:, 1] = zu
    tables["wz"] = wz

    xmom = np.zeros((members[0], 2, 4, SUB, east), np.float32)
    for kind, w in enumerate((ux, vx)):
        for slot in range(4):
            xmom[:, kind, slot, slot] = w.reshape(members[0], east)
    tables["xmom"] = xmom
    return tables


def at(axis, index):
    return {axis: index}


def greet(partners):
    barrier = pltpu.get_barrier_semaphore()
    for partner in partners:
        pl.semaphore_signal(barrier, inc=1, device_id=partner, device_id_type=MESH)
    pl.semaphore_wait(barrier, len(partners))


def remote(src, dst, send, recv, partner):
    return pltpu.make_async_remote_copy(
        src_ref=src, dst_ref=dst, send_sem=send, recv_sem=recv, device_id=partner, device_id_type=MESH
    )


def halo_kernel(sizes, shape, u_ref, hx_ref, hy_ref, send, recv):
    gx, gy = lax.axis_index("gx"), lax.axis_index("gy")
    nx, ny, _ = sizes
    east, north, _ = shape
    xr, xl = lax.rem(gx + 1, nx), lax.rem(gx + nx - 1, nx)
    yr, yl = lax.rem(gy + 1, ny), lax.rem(gy + ny - 1, ny)
    greet([at("gx", xr), at("gx", xl), at("gy", yr), at("gy", yl)])
    copies = [
        remote(u_ref.at[:, north - 1, :], hy_ref.at[0], send.at[2], recv.at[2], at("gy", yr)),
        remote(u_ref.at[:, 0, :], hy_ref.at[1], send.at[3], recv.at[3], at("gy", yl)),
        remote(u_ref.at[east - 1], hx_ref.at[0], send.at[0], recv.at[0], at("gx", xr)),
        remote(u_ref.at[0], hx_ref.at[1], send.at[1], recv.at[1], at("gx", xl)),
    ]
    for copy in copies:
        copy.start()
    for copy in copies:
        copy.wait()


def exchange_halos(u, sizes):
    east, north, upward = u.shape
    vmem = pl.BlockSpec(memory_space=pltpu.VMEM)
    return pl.pallas_call(
        functools.partial(halo_kernel, sizes, u.shape),
        name="halos",
        out_shape=(
            jax.ShapeDtypeStruct((2, north, upward), F32),
            jax.ShapeDtypeStruct((2, east, upward), F32),
        ),
        in_specs=[pl.BlockSpec(memory_space=pl.ANY)],
        out_specs=(vmem, vmem),
        scratch_shapes=[pltpu.SemaphoreType.DMA((4,)), pltpu.SemaphoreType.DMA((4,))],
        compiler_params=pltpu.CompilerParams(collective_id=0, has_side_effects=True),
    )(u)


PLANES = 8
CHUNK = 8


def local_kernel(
    sizes, shape, factors,
    u_ref, s_ref, hx_ref, hy_ref, bzh_ref, bzl_ref, zmom_ref, ytab_ref, xtab_ref,
    g_ref, mx_ref, my_ref, mz_ref,
    u_v, s_v, usem, ssem, gsem,
):
    gx, gy, gz = lax.axis_index("gx"), lax.axis_index("gy"), lax.axis_index("gz")
    nx, ny, _ = sizes
    east, north, upward = shape
    tiles = upward // LANES
    steps = north // SUB
    chunks = east // CHUNK
    rx, ry, _ = factors

    def lanes(l):
        return pl.ds(l * LANES, LANES)

    def loads(c):
        out = []
        rows = pl.ds(c * CHUNK, CHUNK)
        for l in range(tiles):
            out.append(pltpu.make_async_copy(
                u_ref.at[rows, :, lanes(l)], u_v.at[l, pl.ds(1 + c * CHUNK, CHUNK)], usem.at[l, c]))
            out.append(pltpu.make_async_copy(
                s_ref.at[rows, :, lanes(l)], s_v.at[l, rows], ssem.at[l, c]))
        return out

    def stores(c):
        rows = pl.ds(c * CHUNK, CHUNK)
        return [pltpu.make_async_copy(s_v.at[l, rows], g_ref.at[l, rows], gsem.at[l, c]) for l in range(tiles)]

    for c in range(chunks):
        for copy in loads(c):
            copy.start()

    before = jnp.where(gx > 0, 1.0, 0.0).astype(F32)
    after = jnp.where(gx < nx - 1, 1.0, 0.0).astype(F32)
    south = jnp.where(gy > 0, 1.0, 0.0).astype(F32)
    nord = jnp.where(gy < ny - 1, 1.0, 0.0).astype(F32)
    for l in range(tiles):
        u_v[l, 0] = hx_ref[0, :, l * LANES:(l + 1) * LANES] * before
        u_v[l, east + 1] = hx_ref[1, :, l * LANES:(l + 1) * LANES] * after
    mx_ref[...] = jnp.zeros_like(mx_ref)

    bzh, bzl = bzh_ref[gz], bzl_ref[gz]
    zmom = zmom_ref[gz]
    sub = lax.broadcasted_iota(jnp.int32, (SUB, LANES), 0)

    def rows_of(ref, l, i):
        return [ref[l, i, pl.ds(t, SUB, stride=steps), :] for t in range(steps)]

    def stack_rows(rows):
        out = jnp.zeros((SUB, LANES), F32)
        for p, row in enumerate(rows):
            out = jnp.where(sub == p, row, out)
        return out

    def step(b, carry):
        base = pl.multiple_of(b * PLANES, PLANES)
        high, low = [], []
        halo = [
            [hy_ref[side, pl.ds(base, PLANES), l * LANES:(l + 1) * LANES] for l in range(tiles)]
            for side in range(2)
        ]
        for p in range(PLANES):
            i = base + p
            parts = []
            for l in range(tiles):
                col = slice(l * LANES, (l + 1) * LANES)
                u = rows_of(u_v, l, i + 1)
                um = rows_of(u_v, l, i)
                up = rows_of(u_v, l, i + 2)
                s = rows_of(s_v, l, i)
                first = halo[0][l][p:p + 1] * south
                last = halo[1][l][p:p + 1] * nord
                below = jnp.where(sub == 0, first, pltpu.roll(u[-1], 1, 0))
                above = jnp.where(sub == SUB - 1, last, pltpu.roll(u[0], SUB - 1, 0))
                ext = [below] + u + [above]
                f = [
                    s[t] + (2.0 - 2.0 * rx - 2.0 * ry) * u[t]
                    + rx * (um[t] + up[t]) + ry * (ext[t] + ext[t + 2])
                    for t in range(steps)
                ]
                parts.append(jnp.concatenate(f, 0))
            plane = jnp.concatenate(parts, 1)
            h, w = split(plane)
            high.append(h)
            low.append(w)
        high = jnp.concatenate(high, 0)
        low = jnp.concatenate(low, 0)
        y = (
            jnp.dot(high, bzl, preferred_element_type=F32)
            + jnp.dot(low, bzh, preferred_element_type=F32)
            + jnp.dot(high, bzh, preferred_element_type=F32)
        )
        nt = (((1,), (1,)), ((), ()))
        mom = (
            lax.dot_general(zmom, high, nt, preferred_element_type=F32)
            + lax.dot_general(zmom, low, nt, preferred_element_type=F32)
        )
        mu = mom[0:1] + mom[1:2]
        mv = mom[2:3] + mom[3:4]
        for kind, m in enumerate((mu, mv)):
            mz_ref[kind, pl.ds(base, PLANES), :] = stack_rows(
                [m[:, p * north:(p + 1) * north] for p in range(PLANES)])
        for l in range(tiles):
            col = slice(l * LANES, (l + 1) * LANES)
            sums = [[jnp.zeros((SUB, LANES), F32) for _ in range(PLANES)] for _ in range(2)]
            for t in range(steps):
                row = slice(t * SUB, (t + 1) * SUB)
                wu, wv = ytab_ref[gy, 0, row], ytab_ref[gy, 1, row]
                acc_u, acc_v = mx_ref[0, row, col], mx_ref[1, row, col]
                for p in range(PLANES):
                    i = base + p
                    own = u_v[l, i + 1, pl.ds(t, SUB, stride=steps), :]
                    g = y[p * north + t * SUB:p * north + (t + 1) * SUB, col] - 2.0 * own
                    s_v[l, i, row] = g
                    sums[0][p] = sums[0][p] + wu * g
                    sums[1][p] = sums[1][p] + wv * g
                    acc_u = acc_u + xtab_ref[0, gx * east + i] * g
                    acc_v = acc_v + xtab_ref[1, gx * east + i] * g
                mx_ref[0, row, col] = acc_u
                mx_ref[1, row, col] = acc_v
            for kind in range(2):
                my_ref[kind, pl.ds(base, PLANES), col] = stack_rows(
                    [jnp.sum(sums[kind][p], 0, keepdims=True) for p in range(PLANES)])
        return carry

    def chunk(c, carry):
        @pl.when(c < chunks - 1)
        def _():
            for copy in loads(c + 1):
                copy.wait()

        lax.fori_loop(c * (CHUNK // PLANES), (c + 1) * (CHUNK // PLANES), step, 0)
        for copy in stores(c):
            copy.start()
        return carry

    for copy in loads(0):
        copy.wait()
    lax.fori_loop(0, chunks, chunk, 0)
    for c in range(chunks):
        for copy in stores(c):
            copy.wait()


def local_pass(u, s, hx, hy, tables, sizes):
    east, north, upward = u.shape
    tiles = upward // LANES
    chunks = east // CHUNK
    vmem = pl.BlockSpec(memory_space=pltpu.VMEM)
    smem = pl.BlockSpec(memory_space=pltpu.SMEM)
    hbm = pl.BlockSpec(memory_space=pl.ANY)
    return pl.pallas_call(
        functools.partial(local_kernel, sizes, u.shape, tables["factors"]),
        name="local",
        out_shape=(
            jax.ShapeDtypeStruct((tiles, east, north, LANES), F32),
            jax.ShapeDtypeStruct((2, north, upward), F32),
            jax.ShapeDtypeStruct((2, east, upward), F32),
            jax.ShapeDtypeStruct((2, east, north), F32),
        ),
        in_specs=[hbm, hbm, vmem, vmem, vmem, vmem, vmem, vmem, smem],
        out_specs=(hbm, vmem, vmem, vmem),
        scratch_shapes=[
            pltpu.VMEM((tiles, east + 2, north, LANES), F32),
            pltpu.VMEM((tiles, east, north, LANES), F32),
            pltpu.SemaphoreType.DMA((tiles, chunks)),
            pltpu.SemaphoreType.DMA((tiles, chunks)),
            pltpu.SemaphoreType.DMA((tiles, chunks)),
        ],
    )(u, s, hx, hy, tables["bzh"], tables["bzl"], tables["zmom"], tables["y"], tables["x"])


def couple_kernel(
    sizes, shape,
    mx_ref, my_ref, mz_ref, ymom_ref, wy_ref, wz_ref, by_ref, xmom_ref,
    cz_ref, cy_ref, cx_ref,
    zbuf, ybuf, xpair, xtot, xbuf, xback, eown, ebuf, town, tbuf,
    zs, zr, ys, yr, ps, pr, xs, xr, bs, br, es, er, ts, tr,
):
    gx, gy, gz = lax.axis_index("gx"), lax.axis_index("gy"), lax.axis_index("gz")
    nx, ny, nz = sizes
    east, north, upward = shape
    chips = nx // 2
    half = north // 2
    chip, core = gx // 2, lax.rem(gx, 2)
    mine = pl.ds(pl.multiple_of(core * half, half), half)
    theirs = pl.ds(pl.multiple_of((1 - core) * half, half), half)
    partner = at("gx", chip * 2 + 1 - core)

    def ring(axis, me, count):
        return [at(axis, lax.rem(me + o, count)) for o in range(1, count)]

    greet(ring("gx", gx, nx) + ring("gy", gy, ny) + ring("gz", gz, nz))

    def kind_to(me, count, o):
        return jnp.where(lax.rem(me + o, count) > me, 0, 1)

    def from_below(me, count, o):
        return jnp.where(lax.rem(me + count - o, count) < me, 1.0, 0.0).astype(F32)

    def gather(me, count, buf):
        left = right = None
        for o in range(1, count):
            low = from_below(me, count, o)
            piece = buf[o - 1]
            left = piece * low if left is None else left + piece * low
            right = piece * (1.0 - low) if right is None else right + piece * (1.0 - low)
        return left, right

    pair = remote(mx_ref.at[:, theirs, :], xpair, ps, pr, partner)
    pair.start()
    zcopies = [
        remote(mz_ref.at[kind_to(gz, nz, o)], zbuf.at[o - 1], zs.at[o - 1], zr.at[o - 1],
               at("gz", lax.rem(gz + o, nz)))
        for o in range(1, nz)
    ]
    for copy in zcopies:
        copy.start()
    ycopies = [
        remote(my_ref.at[kind_to(gy, ny, o)], ybuf.at[o - 1], ys.at[o - 1], yr.at[o - 1],
               at("gy", lax.rem(gy + o, ny)))
        for o in range(1, ny)
    ]
    for copy in ycopies:
        copy.start()
    pair.wait()
    xtot[0] = mx_ref[0, mine, :] + xpair[0]
    xtot[1] = mx_ref[1, mine, :] + xpair[1]
    xcopies = [
        remote(xtot.at[kind_to(chip, chips, o)], xbuf.at[o - 1], xs.at[o - 1], xr.at[o - 1],
               at("gx", lax.rem(chip + o, chips) * 2 + core))
        for o in range(1, chips)
    ]
    for copy in xcopies:
        copy.start()

    for copy in zcopies:
        copy.wait()
    pz, sz = gather(gz, nz, zbuf)

    def pack(value, base):
        high = value.astype(BF16).astype(F32)
        low = (value - high).astype(BF16).astype(F32)
        cz_ref[:, base, :] = high
        cz_ref[:, base + 1, :] = low
        cz_ref[:, base + 2, :] = high

    pack(pz, 0)
    pack(sz, 3)
    cz_ref[:, 6, :] = jnp.zeros_like(pz)
    cz_ref[:, 7, :] = jnp.zeros_like(pz)

    def dot(a, b, dims=(((1,), (0,)), ((), ()))):
        return lax.dot_general(a, b, dims, precision=HIGH, preferred_element_type=F32)

    for kind in range(2):
        eown[kind] = dot(pz, ymom_ref[gy, kind, 0]) + dot(sz, ymom_ref[gy, kind, 1])
    ecopies = [
        remote(eown.at[kind_to(gy, ny, o)], ebuf.at[o - 1], es.at[o - 1], er.at[o - 1],
               at("gy", lax.rem(gy + o, ny)))
        for o in range(1, ny)
    ]
    for copy in ecopies:
        copy.start()

    for copy in ycopies:
        copy.wait()
    left, right = gather(gy, ny, ybuf)
    for copy in ecopies:
        copy.wait()
    eleft, eright = gather(gy, ny, ebuf)
    wz = wz_ref[gz]
    py = left + dot(eleft, wz)
    sy = right + dot(eright, wz)
    cy_ref[0] = py
    cy_ref[1] = sy

    for kind in range(2):
        town[kind, :, 0:upward] = (
            dot(xmom_ref[gx, kind, 0], py) + dot(xmom_ref[gx, kind, 1], sy))
        town[kind, :, upward:] = (
            dot(xmom_ref[gx, kind, 0], pz) + dot(xmom_ref[gx, kind, 1], sz))
    tcopies = [
        remote(town.at[kind_to(gx, nx, o)], tbuf.at[o - 1], ts.at[o - 1], tr.at[o - 1],
               at("gx", lax.rem(gx + o, nx)))
        for o in range(1, nx)
    ]
    for copy in tcopies:
        copy.start()

    for copy in xcopies:
        copy.wait()
    px, sx = gather(chip, chips, xbuf)
    first = jnp.where(core == 0, 1.0, 0.0).astype(F32)
    second = 1.0 - first
    xback[0] = px + first * mx_ref[0, mine, :]
    xback[1] = sx + second * mx_ref[1, mine, :]
    back = remote(xback, cx_ref.at[:, mine, :], bs, br, partner)
    back.start()
    cx_ref[0, mine, :] = px + second * xpair[0]
    cx_ref[1, mine, :] = sx + first * xpair[1]

    for copy in tcopies:
        copy.wait()
    tleft, tright = gather(gx, nx, tbuf)
    tright = tright + town[1]
    by = by_ref[gy]
    wy = wy_ref[gy][:, 0:SUB]
    back.wait()
    for kind, edge in ((0, tleft), (1, tright)):
        face = cx_ref[kind]
        if kind == 1:
            face = face + mx_ref[1]
        folded = dot(edge[:, upward:], by)
        cx_ref[kind] = (
            dot(by, face)
            + dot(wy, edge[:, 0:upward])
            + dot(folded, wz[0:SUB], (((0,), (0,)), ((), ())))
        )


def couple(mx, my, mz, tables, shape, sizes):
    east, north, upward = shape
    nx, ny, nz = sizes
    chips = nx // 2
    vmem = pl.BlockSpec(memory_space=pltpu.VMEM)
    dma = pltpu.SemaphoreType.DMA
    half = north // 2
    return pl.pallas_call(
        functools.partial(couple_kernel, sizes, shape),
        name="couple",
        out_shape=(
            jax.ShapeDtypeStruct((east, SUB, north), F32),
            jax.ShapeDtypeStruct((2, east, upward), F32),
            jax.ShapeDtypeStruct((2, north, upward), F32),
        ),
        in_specs=[vmem] * 8,
        out_specs=(vmem, vmem, vmem),
        scratch_shapes=[
            pltpu.VMEM((nz - 1, east, north), F32),
            pltpu.VMEM((ny - 1, east, upward), F32),
            pltpu.VMEM((2, half, upward), F32),
            pltpu.VMEM((2, half, upward), F32),
            pltpu.VMEM((chips - 1, half, upward), F32),
            pltpu.VMEM((2, half, upward), F32),
            pltpu.VMEM((2, east, LANES), F32),
            pltpu.VMEM((ny - 1, east, LANES), F32),
            pltpu.VMEM((2, SUB, upward + north), F32),
            pltpu.VMEM((nx - 1, SUB, upward + north), F32),
            dma((nz - 1,)), dma((nz - 1,)),
            dma((ny - 1,)), dma((ny - 1,)),
            dma, dma,
            dma((chips - 1,)), dma((chips - 1,)),
            dma, dma,
            dma((ny - 1,)), dma((ny - 1,)),
            dma((nx - 1,)), dma((nx - 1,)),
        ],
        compiler_params=pltpu.CompilerParams(collective_id=1, has_side_effects=True),
    )(mx, my, mz, tables["ymom"], tables["wy"], tables["wz"], tables["by"], tables["xmom"])


def final_kernel(
    shape,
    g_ref, u_ref, cz_ref, cy_ref, cx_ref, zadd_ref, ytab_ref, xtab_ref,
    o_ref,
    g_v, u_v, o_v, gsem, usem, osem,
):
    gx, gy, gz = lax.axis_index("gx"), lax.axis_index("gy"), lax.axis_index("gz")
    east, north, upward = shape
    tiles = upward // LANES
    steps = north // SUB
    chunks = east // CHUNK

    def lanes(l):
        return pl.ds(l * LANES, LANES)

    def loads(c):
        out = []
        rows = pl.ds(c * CHUNK, CHUNK)
        for l in range(tiles):
            out.append(pltpu.make_async_copy(g_ref.at[l, rows], g_v.at[l, rows], gsem.at[l, c]))
            out.append(pltpu.make_async_copy(
                u_ref.at[rows, :, lanes(l)], u_v.at[l, rows], usem.at[l, c]))
        return out

    def stores(c):
        rows = pl.ds(c * CHUNK, CHUNK)
        return [
            pltpu.make_async_copy(o_v.at[l, rows], o_ref.at[rows, :, lanes(l)], osem.at[l, c])
            for l in range(tiles)
        ]

    for c in range(chunks):
        for copy in loads(c):
            copy.start()

    zadd = zadd_ref[gz]
    sub = lax.broadcasted_iota(jnp.int32, (SUB, LANES), 0)

    def scan(value, backward):
        def shifted(x, d):
            if backward:
                return jnp.where(sub < SUB - d, pltpu.roll(x, SUB - d, 0), 0.0)
            return jnp.where(sub >= d, pltpu.roll(x, d, 0), 0.0)

        for d in (1, 2, 4):
            value = value + shifted(value, d)
        return shifted(value, 1)

    def step(b, carry):
        base = pl.multiple_of(b * PLANES, PLANES)
        add = []
        for p in range(PLANES):
            cz = cz_ref[base + p].T.astype(BF16)
            add.append(jnp.dot(cz, zadd, preferred_element_type=F32))
        for l in range(tiles):
            col = slice(l * LANES, (l + 1) * LANES)
            edge = [cy_ref[kind, pl.ds(base, PLANES), col] for kind in range(2)]
            for p in range(PLANES):
                i = base + p
                g = []
                for t in range(steps):
                    row = slice(t * SUB, (t + 1) * SUB)
                    g.append(g_v[l, i, row] + add[p][row, col])
                su = sv = None
                for t in range(steps):
                    row = slice(t * SUB, (t + 1) * SUB)
                    pu = ytab_ref[gy, 0, row] * g[t]
                    pv = ytab_ref[gy, 1, row] * g[t]
                    su = pu if su is None else su + pu
                    sv = pv if sv is None else sv + pv
                below = scan(su, False) + edge[0][p:p + 1]
                above = scan(sv, True) + edge[1][p:p + 1] + sv
                for t in range(steps):
                    row = slice(t * SUB, (t + 1) * SUB)
                    wu, wv = ytab_ref[gy, 0, row], ytab_ref[gy, 1, row]
                    below = below + wu * g[t]
                    above = above - wv * g[t]
                    g_v[l, i, row] = wv * below + wu * above
            for t in range(steps):
                row = slice(t * SUB, (t + 1) * SUB)
                below, above = cx_ref[0, row, col], cx_ref[1, row, col]
                for p in range(PLANES):
                    i = base + p
                    wu, wv = xtab_ref[0, gx * east + i], xtab_ref[1, gx * east + i]
                    h = g_v[l, i, row]
                    below = below + wu * h
                    above = above - wv * h
                    own = u_v[l, i, pl.ds(t, SUB, stride=steps), :]
                    o_v[l, i, pl.ds(t, SUB, stride=steps), :] = own + (wv * below + wu * above)
                cx_ref[0, row, col] = below
                cx_ref[1, row, col] = above
        return carry

    def chunk(c, carry):
        for copy in loads(c):
            copy.wait()
        lax.fori_loop(c * (CHUNK // PLANES), (c + 1) * (CHUNK // PLANES), step, 0)
        for copy in stores(c):
            copy.start()
        return carry

    lax.fori_loop(0, chunks, chunk, 0)
    for c in range(chunks):
        for copy in stores(c):
            copy.wait()


def final_outer(shape, g_ref, u_ref, cz_ref, cy_ref, cxin_ref, zadd_ref, ytab_ref, xtab_ref, o_ref, cx_v, *rest):
    cx_v[...] = cxin_ref[...]
    final_kernel(shape, g_ref, u_ref, cz_ref, cy_ref, cx_v, zadd_ref, ytab_ref, xtab_ref, o_ref, *rest)


def final_pass(g, u, cz, cy, cx, tables):
    east, north, upward = u.shape
    tiles = upward // LANES
    chunks = east // CHUNK
    vmem = pl.BlockSpec(memory_space=pltpu.VMEM)
    smem = pl.BlockSpec(memory_space=pltpu.SMEM)
    hbm = pl.BlockSpec(memory_space=pl.ANY)
    block = pltpu.VMEM((tiles, east, north, LANES), F32)
    return pl.pallas_call(
        functools.partial(final_outer, u.shape),
        name="final",
        out_shape=jax.ShapeDtypeStruct(u.shape, F32),
        in_specs=[hbm, hbm, vmem, vmem, vmem, vmem, vmem, smem],
        out_specs=hbm,
        scratch_shapes=[
            pltpu.VMEM((2, north, upward), F32),
            block, block, block,
            pltpu.SemaphoreType.DMA((tiles, chunks)),
            pltpu.SemaphoreType.DMA((tiles, chunks)),
            pltpu.SemaphoreType.DMA((tiles, chunks)),
        ],
    )(g, u, cz, cy, cx, tables["zadd"], tables["y"], tables["x"])


def local(sizes, u, s):
    tables = make_tables(u.shape, sizes)
    hx, hy = exchange_halos(u, sizes)
    g, mx, my, mz = local_pass(u, s, hx, hy, tables, sizes)
    cz, cy, cx = couple(mx, my, mz, tables, u.shape, sizes)
    return final_pass(g, u, cz, cy, cx, tables)


def solution(mesh):
    sizes = tuple(mesh.shape[name] for name in ("gx", "gy", "gz"))
    spec = P("gx", "gy", "gz")
    return jax.shard_map(
        functools.partial(local, sizes), mesh=mesh, in_specs=(spec, spec), out_specs=spec, check_vma=False
    )
```

```python
import functools

import jax
import jax.numpy as jnp
import numpy as np
from jax import lax
from jax.experimental import pallas as pl
from jax.experimental.pallas import tpu as pltpu
from jax.sharding import PartitionSpec as P

MESH = pl.DeviceIdType.MESH
HIGH = lax.Precision.HIGHEST
F32 = jnp.float32
BF16 = jnp.bfloat16
LANES = 128
SUB = 8


def generators(whole, factor):
    half = 0.5 * factor
    theta = np.arccosh(1.0 + 0.5 / half)
    scale = np.sqrt(1.0 / (half * np.sinh(theta) * np.sinh((whole + 1) * theta)))
    index = np.arange(whole, dtype=np.float64)
    return np.sinh((index + 1) * theta) * scale, np.sinh((whole - index) * theta) * scale


def diagonal_blocks(u, v, members):
    extent = u.shape[0] // members
    blocks = []
    for member in range(members):
        part = slice(member * extent, (member + 1) * extent)
        own_u, own_v = u[part], v[part]
        lower = np.outer(own_v, own_u)
        blocks.append(np.where(np.tri(extent, dtype=bool), lower, lower.T))
    return np.stack(blocks)


def split_bf16(values):
    high = values.astype(np.float32).astype(BF16)
    low = (values - high.astype(np.float64)).astype(np.float32).astype(BF16)
    return np.asarray(high), np.asarray(low)


def split(values):
    high = values.astype(BF16)
    return high, (values - high.astype(F32)).astype(BF16)


def make_tables(shape, members):
    east, north, upward = shape
    wholes = [extent * count for extent, count in zip(shape, members)]
    factors = [float(whole * whole // 4) for whole in wholes]
    order = np.arange(north)
    order = (north // SUB) * (order % SUB) + order // SUB

    ux, vx = generators(wholes[0], factors[0])
    uy, vy = generators(wholes[1], factors[1])
    uz, vz = generators(wholes[2], factors[2])
    tables = {"factors": factors}
    tables["x"] = np.stack([ux, vx]).astype(np.float32)

    own = np.stack([w.reshape(members[1], north)[:, order] for w in (uy, vy)], 1)
    tables["y"] = np.repeat(own[..., None], LANES, -1).astype(np.float32)
    by = diagonal_blocks(uy, vy, members[1])[:, order][:, :, order]
    tables["by"] = by.astype(np.float32)
    tables["bx"] = diagonal_blocks(ux, vx, members[0]).astype(np.float32)
    yw = np.zeros((members[1], 2, 2, SUB, north), np.float32)
    xw = np.zeros((members[0], 2, 2, SUB, east), np.float32)
    for slot in range(2):
        yw[:, :, slot, slot] = own
        for kind, w in enumerate((ux, vx)):
            xw[:, kind, slot, slot] = w.reshape(members[0], east)
    tables["yw"], tables["xw"] = yw, xw
    wy = np.zeros((members[1], SUB, north), np.float32)
    wy[:, 0] = own[:, 1]
    wy[:, 1] = own[:, 0]
    tables["wy"] = wy

    bzh, bzl = split_bf16(diagonal_blocks(uz, vz, members[2]))
    tables["bz"] = np.stack([bzh, bzl], 1)
    zu, zv = uz.reshape(members[2], upward), vz.reshape(members[2], upward)
    uh, ul = split_bf16(zu)
    vh, vl = split_bf16(zv)
    zero = np.zeros_like(uh)
    tables["zmom"] = np.stack([uh, ul, vh, vl] + [zero] * 12, 1)
    tables["zadd"] = np.stack([vh, vh, vl, uh, uh, ul, zero, zero], 1)
    return tables


def at(axis, index):
    return {axis: index}


def greet(partners):
    barrier = pltpu.get_barrier_semaphore()
    for partner in partners:
        pl.semaphore_signal(barrier, inc=1, device_id=partner, device_id_type=MESH)
    pl.semaphore_wait(barrier, len(partners))


def remote(src, dst, send, recv, partner):
    return pltpu.make_async_remote_copy(
        src_ref=src, dst_ref=dst, send_sem=send, recv_sem=recv, device_id=partner, device_id_type=MESH
    )


def kind_to(me, count, o):
    return jnp.where(lax.rem(me + o, count) > me, 0, 1)


def gather(me, count, buf):
    left = right = None
    for o in range(1, count):
        low = jnp.where(lax.rem(me + count - o, count) < me, 1.0, 0.0).astype(F32)
        piece = buf[o - 1]
        left = piece * low if left is None else left + piece * low
        right = piece * (1.0 - low) if right is None else right + piece * (1.0 - low)
    return left, right


NN = (((1,), (0,)), ((), ()))
NT = (((1,), (1,)), ((), ()))
TN = (((0,), (0,)), ((), ()))


def dot(a, b, dims=NN):
    return lax.dot_general(a, b, dims, precision=HIGH, preferred_element_type=F32)


PLANES = 8


def stack_rows(rows, width=LANES):
    sub = lax.broadcasted_iota(jnp.int32, (SUB, width), 0)
    out = jnp.zeros((SUB, width), F32)
    for p, row in enumerate(rows):
        out = jnp.where(sub == p, row, out)
    return out


def local_kernel(
    sizes, shape, factors,
    u_ref, s_ref, bz_ref, zmom_ref, ytab_ref, yw_ref, xw_ref, wy_ref, by_ref, bx_ref, xtab_ref,
    g_ref, sg_ref, cz_ref, cy_ref, cx_ref,
    u_v, s_v, fh, fl, hx, hy, mxf, mxu, mx, my, mz,
    zbuf, zpad, ybuf, xpair, xtot, xbuf, xback, eown, ebuf, qown, qbuf, rown, rbuf, town, tbuf,
    usem, ssem, gsem, hs, hr, zs, zr, ys, yr, ps, pr, xs, xr, bs, br, es, er, qs, qr, rs, rr, ts, tr,
):
    gx, gy, gz = lax.axis_index("gx"), lax.axis_index("gy"), lax.axis_index("gz")
    nx, ny, nz = sizes
    east, north, upward = shape
    tiles = upward // LANES
    steps = north // SUB
    chunks = east // PLANES
    rx, ry, _ = factors
    chips = nx // 2
    half = north // 2
    chip, core = gx // 2, lax.rem(gx, 2)
    mine = pl.ds(pl.multiple_of(core * half, half), half)
    theirs = pl.ds(pl.multiple_of((1 - core) * half, half), half)
    partner = at("gx", chip * 2 + 1 - core)

    def lanes(l):
        return pl.ds(l * LANES, LANES)

    def u_loads(c):
        rows = pl.ds(c * PLANES, PLANES)
        return [
            pltpu.make_async_copy(
                u_ref.at[rows, :, lanes(l)], u_v.at[l, pl.ds(1 + c * PLANES, PLANES)], usem.at[l, c])
            for l in range(tiles)
        ]

    def s_loads(c):
        rows = pl.ds(c * PLANES, PLANES)
        return [
            pltpu.make_async_copy(s_ref.at[rows, :, lanes(l)], s_v.at[l, rows], ssem.at[l, c])
            for l in range(tiles)
        ]

    def g_stores(c):
        rows = pl.ds(c * PLANES, PLANES)
        return [pltpu.make_async_copy(s_v.at[l, rows], g_ref.at[l, rows], gsem.at[l, c]) for l in range(tiles)]

    for loads in (u_loads, s_loads):
        for c in range(chunks):
            for copy in loads(c):
                copy.start()

    def ring(axis, me, count):
        return [at(axis, lax.rem(me + o, count)) for o in range(1, count)]

    greet(ring("gx", gx, nx) + ring("gy", gy, ny) + ring("gz", gz, nz))

    xr_, xl_ = lax.rem(gx + 1, nx), lax.rem(gx + nx - 1, nx)
    yr_, yl_ = lax.rem(gy + 1, ny), lax.rem(gy + ny - 1, ny)
    halos = [
        remote(u_ref.at[:, north - 1, :], hy.at[0], hs.at[2], hr.at[2], at("gy", yr_)),
        remote(u_ref.at[:, 0, :], hy.at[1], hs.at[3], hr.at[3], at("gy", yl_)),
        remote(u_ref.at[east - 1], hx.at[0], hs.at[0], hr.at[0], at("gx", xr_)),
        remote(u_ref.at[0], hx.at[1], hs.at[1], hr.at[1], at("gx", xl_)),
    ]
    for copy in halos:
        copy.start()

    sub = lax.broadcasted_iota(jnp.int32, (SUB, LANES), 0)

    def cols(l):
        return slice(l * LANES, (l + 1) * LANES)

    def rows_at(t):
        return slice(t * SUB, (t + 1) * SUB)

    def strided(t):
        return pl.ds(t, SUB, stride=steps)

    mxu[...] = jnp.zeros_like(mxu)
    mxf[...] = jnp.zeros_like(mxf)
    zpad[...] = jnp.zeros_like(zpad)

    def weights(base):
        return [[xtab_ref[kind, gx * east + base + p] for p in range(PLANES)] for kind in range(2)]

    def pre(c, carry):
        for copy in u_loads(c):
            copy.wait()
        base = c * PLANES
        w = weights(base)
        for l in range(tiles):
            for t in range(steps):
                acc = [mxu[kind, rows_at(t), cols(l)] for kind in range(2)]
                for p in range(PLANES):
                    own = u_v[l, base + p + 1, strided(t), :]
                    for kind in range(2):
                        acc[kind] = acc[kind] + w[kind][p] * own
                for kind in range(2):
                    mxu[kind, rows_at(t), cols(l)] = acc[kind]
        return carry

    lax.fori_loop(0, chunks, pre, 0)

    for copy in halos:
        copy.wait()
    before = jnp.where(gx > 0, 1.0, 0.0).astype(F32)
    after = jnp.where(gx < nx - 1, 1.0, 0.0).astype(F32)
    south = jnp.where(gy > 0, 1.0, 0.0).astype(F32)
    nord = jnp.where(gy < ny - 1, 1.0, 0.0).astype(F32)
    for l in range(tiles):
        u_v[l, 0] = hx[0, :, cols(l)] * before
        u_v[l, east + 1] = hx[1, :, cols(l)] * after

    zmom = zmom_ref[gz]

    def z_moments(c):
        base = pl.multiple_of(c * PLANES, PLANES)
        mom = None
        for f in (fh, fl):
            flat = f[pl.ds(base, PLANES)].reshape(PLANES * north, upward)
            part = lax.dot_general(zmom, flat, NT, preferred_element_type=F32)
            mom = part if mom is None else mom + part
        for kind in range(2):
            m = mom[2 * kind:2 * kind + 1] + mom[2 * kind + 1:2 * kind + 2]
            mz[kind, pl.ds(base, PLANES), :] = stack_rows(
                [m[:, p * north:(p + 1) * north] for p in range(PLANES)])

    def rhs(c, carry):
        for copy in s_loads(c):
            copy.wait()
        base = pl.multiple_of(c * PLANES, PLANES)
        w = weights(base)
        for l in range(tiles):
            col = cols(l)
            edge = [hy[0, pl.ds(base, PLANES), col] * south, hy[1, pl.ds(base, PLANES), col] * nord]
            for t2 in range(0, steps, 2):
                acc = [[mxf[kind, rows_at(t2 + k), col] for k in range(2)] for kind in range(2)]
                column = [[u_v[l, base + p, strided(t2 + k), :] for p in range(PLANES + 2)] for k in range(2)]
                for p in range(PLANES):
                    i = base + p
                    if t2 == 0:
                        below = pltpu.roll(u_v[l, i + 1, strided(steps - 1), :], 1, 0)
                        below = jnp.where(sub == 0, edge[0][p:p + 1], below)
                    else:
                        below = u_v[l, i + 1, strided(t2 - 1), :]
                    if t2 == steps - 2:
                        above = pltpu.roll(u_v[l, i + 1, strided(0), :], SUB - 1, 0)
                        above = jnp.where(sub == SUB - 1, edge[1][p:p + 1], above)
                    else:
                        above = u_v[l, i + 1, strided(t2 + 2), :]
                    out = []
                    for k in range(2):
                        own = column[k][p + 1]
                        across = column[k][p] + column[k][p + 2]
                        along = (below + column[1][p + 1]) if k == 0 else (column[0][p + 1] + above)
                        if rx == ry:
                            spread = rx * ((across + along) + (2.0 / rx - 4.0) * own)
                        else:
                            spread = rx * across + ry * along + (2.0 - 2.0 * rx - 2.0 * ry) * own
                        f = s_v[l, i, strided(t2 + k), :] + spread
                        for kind in range(2):
                            acc[kind][k] = acc[kind][k] + w[kind][p] * f
                        out.append(f)
                    pair = jnp.concatenate(out, 0)
                    high = pair.astype(BF16)
                    rows = slice(t2 * SUB, (t2 + 2) * SUB)
                    fh[i, rows, col] = high
                    fl[i, rows, col] = (pair - high.astype(F32)).astype(BF16)
                for kind in range(2):
                    for k in range(2):
                        mxf[kind, rows_at(t2 + k), col] = acc[kind][k]
        z_moments(c)
        return carry

    lax.fori_loop(0, chunks, rhs, 0)

    zcopies = [
        remote(mz.at[kind_to(gz, nz, o)], zbuf.at[o - 1], zs.at[o - 1], zr.at[o - 1],
               at("gz", lax.rem(gz + o, nz)))
        for o in range(1, nz)
    ]
    for copy in zcopies:
        copy.start()

    def solve_up(high, low):
        stack = jnp.concatenate([bz_ref[gz, 1], bz_ref[gz, 0], bz_ref[gz, 0]], 0)
        return jnp.dot(jnp.concatenate([high, low, high], 1), stack, preferred_element_type=F32)

    fold_h, fold_l = split(mxf[...].reshape(2 * north, upward))
    mx[...] = solve_up(fold_h, fold_l).reshape(2, north, upward) - 2.0 * mxu[...]

    pair = remote(mx.at[:, theirs, :], xpair, ps, pr, partner)
    pair.start()
    for kind in range(2):
        qown[kind] = dot(yw_ref[gy, kind, 0], mx[0]) + dot(yw_ref[gy, kind, 1], mx[1])
    qcopies = [
        remote(qown.at[kind_to(gy, ny, o)], qbuf.at[o - 1], qs.at[o - 1], qr.at[o - 1],
               at("gy", lax.rem(gy + o, ny)))
        for o in range(1, ny)
    ]
    for copy in qcopies:
        copy.start()
    xcopies = [
        remote(xtot.at[kind_to(chip, chips, o)], xbuf.at[o - 1], xs.at[o - 1], xr.at[o - 1],
               at("gx", lax.rem(chip + o, chips) * 2 + core))
        for o in range(1, chips)
    ]
    rcopies = [
        remote(rown.at[kind_to(gx, nx, o)], rbuf.at[o - 1], rs.at[o - 1], rr.at[o - 1],
               at("gx", lax.rem(gx + o, nx)))
        for o in range(1, nx)
    ]

    def send_chips():
        pair.wait()
        xtot[0] = mx[0, mine, :] + xpair[0]
        xtot[1] = mx[1, mine, :] + xpair[1]
        for copy in xcopies:
            copy.start()

    def send_edges():
        for copy in qcopies:
            copy.wait()
        qleft, qright = gather(gy, ny, qbuf)
        for kind in range(2):
            rown[kind] = stack_rows([qleft[kind:kind + 1], qright[kind:kind + 1]], upward)
        for copy in rcopies:
            copy.start()

    def solve(c, carry):
        base = pl.multiple_of(c * PLANES, PLANES)

        @pl.when(c == min(2, chunks - 1))
        def _():
            send_chips()

        @pl.when(c == min(5, chunks - 1))
        def _():
            send_edges()

        y = solve_up(
            fh[pl.ds(base, PLANES)].reshape(PLANES * north, upward),
            fl[pl.ds(base, PLANES)].reshape(PLANES * north, upward),
        )
        for l in range(tiles):
            col = cols(l)
            sums = [[None] * PLANES for _ in range(2)]
            for t in range(steps):
                w = [ytab_ref[gy, kind, rows_at(t)] for kind in range(2)]
                for p in range(PLANES):
                    i = base + p
                    own = u_v[l, i + 1, strided(t), :]
                    g = y[p * north + t * SUB:p * north + (t + 1) * SUB, col] - 2.0 * own
                    s_v[l, i, rows_at(t)] = g
                    for kind in range(2):
                        term = w[kind] * g
                        sums[kind][p] = term if t == 0 else sums[kind][p] + term
            for kind in range(2):
                for p in range(PLANES):
                    sg_ref[kind, base + p, :, col] = sums[kind][p]
                my[kind, pl.ds(base, PLANES), col] = stack_rows(
                    [jnp.sum(sums[kind][p], 0, keepdims=True) for p in range(PLANES)])
        for copy in g_stores(c):
            copy.start()
        return carry

    lax.fori_loop(0, chunks, solve, 0)

    for copy in zcopies:
        copy.wait()
    coef = gather(gz, nz, zbuf)
    for m in range(2):
        zpad[m, 0:east] = coef[m]
    for kind in range(2):
        eown[kind] = dot(yw_ref[gy, kind, 0], zpad[0], NT) + dot(yw_ref[gy, kind, 1], zpad[1], NT)
    ecopies = [
        remote(eown.at[kind_to(gy, ny, o)], ebuf.at[o - 1], es.at[o - 1], er.at[o - 1],
               at("gy", lax.rem(gy + o, ny)))
        for o in range(1, ny)
    ]
    for copy in ecopies:
        copy.start()
    ycopies = [
        remote(my.at[kind_to(gy, ny, o)], ybuf.at[o - 1], ys.at[o - 1], yr.at[o - 1],
               at("gy", lax.rem(gy + o, ny)))
        for o in range(1, ny)
    ]
    for copy in ycopies:
        copy.start()

    by = by_ref[gy]
    face = [dot(coef[m], by) for m in range(2)]
    for copy in ecopies:
        copy.wait()
    eleft, eright = gather(gy, ny, ebuf)
    for m in range(2):
        face[m] = face[m] + (
            dot(eleft, yw_ref[gy, 1, m], TN) + dot(eright, yw_ref[gy, 0, m], TN))[0:east]
    for kind in range(2):
        town[kind] = dot(xw_ref[gx, kind, 0], face[0]) + dot(xw_ref[gx, kind, 1], face[1])
    tcopies = [
        remote(town.at[kind_to(gx, nx, o)], tbuf.at[o - 1], ts.at[o - 1], tr.at[o - 1],
               at("gx", lax.rem(gx + o, nx)))
        for o in range(1, nx)
    ]
    for copy in tcopies:
        copy.start()
    bx = bx_ref[gx]
    face = [dot(bx, face[m]) for m in range(2)]

    for copy in xcopies:
        copy.wait()
    px, sx = gather(chip, chips, xbuf)
    first = jnp.where(core == 0, 1.0, 0.0).astype(F32)
    second = 1.0 - first
    xback[0] = px + first * mx[0, mine, :]
    xback[1] = sx + second * mx[1, mine, :]
    back = remote(xback, cx_ref.at[:, mine, :], bs, br, partner)
    back.start()
    cx_ref[0, mine, :] = px + second * xpair[0]
    cx_ref[1, mine, :] = sx + first * xpair[1]
    for copy in rcopies:
        copy.wait()
    rleft, rright = gather(gx, nx, rbuf)
    rright = rright + rown[1]
    back.wait()
    wy = wy_ref[gy]
    cx_ref[0] = dot(by, cx_ref[0]) + dot(wy, rleft, TN)
    cx_ref[1] = dot(by, cx_ref[1] + mx[1]) + dot(wy, rright, TN)

    for copy in tcopies:
        copy.wait()
    tleft, tright = gather(gx, nx, tbuf)
    for m in range(2):
        value = face[m] + dot(xw_ref[gx, 1, m], tleft, TN) + dot(xw_ref[gx, 0, m], tright, TN)
        high = value.astype(BF16).astype(F32)
        cz_ref[:, 3 * m, :] = high
        cz_ref[:, 3 * m + 1, :] = (value - high).astype(BF16).astype(F32)
        cz_ref[:, 3 * m + 2, :] = high
        cz_ref[:, 6 + m, :] = jnp.zeros_like(value)

    for copy in ycopies:
        copy.wait()
    left, right = gather(gy, ny, ybuf)
    cy_ref[0] = left
    cy_ref[1] = right
    for c in range(chunks):
        for copy in g_stores(c):
            copy.wait()


def local_pass(u, s, tables, sizes):
    east, north, upward = u.shape
    nx, ny, nz = sizes
    tiles = upward // LANES
    chunks = east // PLANES
    chips = nx // 2
    half = north // 2
    vmem = pl.BlockSpec(memory_space=pltpu.VMEM)
    smem = pl.BlockSpec(memory_space=pltpu.SMEM)
    hbm = pl.BlockSpec(memory_space=pl.ANY)
    dma = pltpu.SemaphoreType.DMA

    def buf(*dims):
        return pltpu.VMEM(dims, F32)

    names = ("bz", "zmom", "y", "yw", "xw", "wy", "by", "bx")
    return pl.pallas_call(
        functools.partial(local_kernel, sizes, u.shape, tables["factors"]),
        name="local",
        out_shape=(
            jax.ShapeDtypeStruct((tiles, east, north, LANES), F32),
            jax.ShapeDtypeStruct((2, east, SUB, upward), F32),
            jax.ShapeDtypeStruct((east, SUB, north), F32),
            jax.ShapeDtypeStruct((2, east, upward), F32),
            jax.ShapeDtypeStruct((2, north, upward), F32),
        ),
        in_specs=[hbm, hbm] + [vmem] * len(names) + [smem],
        out_specs=(hbm, vmem, vmem, vmem, vmem),
        scratch_shapes=[
            buf(tiles, east + 2, north, LANES),
            buf(tiles, east, north, LANES),
            pltpu.VMEM((east, north, upward), BF16),
            pltpu.VMEM((east, north, upward), BF16),
            buf(2, north, upward), buf(2, east, upward),
            buf(2, north, upward), buf(2, north, upward), buf(2, north, upward),
            buf(2, east, upward), buf(2, east, north),
            buf(nz - 1, east, north), buf(2, LANES, north), buf(ny - 1, east, upward),
            buf(2, half, upward), buf(2, half, upward), buf(chips - 1, half, upward), buf(2, half, upward),
            buf(2, SUB, LANES), buf(ny - 1, SUB, LANES),
            buf(2, SUB, upward), buf(ny - 1, SUB, upward),
            buf(2, SUB, upward), buf(nx - 1, SUB, upward),
            buf(2, SUB, north), buf(nx - 1, SUB, north),
            dma((tiles, chunks)), dma((tiles, chunks)), dma((tiles, chunks)),
            dma((4,)), dma((4,)),
            dma((nz - 1,)), dma((nz - 1,)),
            dma((ny - 1,)), dma((ny - 1,)),
            dma, dma,
            dma((chips - 1,)), dma((chips - 1,)),
            dma, dma,
            dma((ny - 1,)), dma((ny - 1,)),
            dma((ny - 1,)), dma((ny - 1,)),
            dma((nx - 1,)), dma((nx - 1,)),
            dma((nx - 1,)), dma((nx - 1,)),
        ],
        compiler_params=pltpu.CompilerParams(collective_id=0, has_side_effects=True),
    )(u, s, *[tables[name] for name in names], tables["x"])


def final_kernel(
    shape,
    g_ref, u_ref, sg_ref, cz_ref, cy_ref, cx_ref, zadd_ref, ytab_ref, xtab_ref,
    o_ref,
    below_v, g_v, u_v, o_v, gsem, usem, osem,
):
    gx, gy, gz = lax.axis_index("gx"), lax.axis_index("gy"), lax.axis_index("gz")
    east, north, upward = shape
    tiles = upward // LANES
    steps = north // SUB
    chunks = east // PLANES

    def lanes(l):
        return pl.ds(l * LANES, LANES)

    def loads(c):
        out = []
        rows = pl.ds(c * PLANES, PLANES)
        for l in range(tiles):
            out.append(pltpu.make_async_copy(g_ref.at[l, rows], g_v.at[l, rows], gsem.at[l, c]))
            out.append(pltpu.make_async_copy(
                u_ref.at[rows, :, lanes(l)], u_v.at[l, rows], usem.at[l, c]))
        return out

    def stores(c):
        rows = pl.ds(c * PLANES, PLANES)
        return [
            pltpu.make_async_copy(o_v.at[l, rows], o_ref.at[rows, :, lanes(l)], osem.at[l, c])
            for l in range(tiles)
        ]

    for c in range(chunks):
        for copy in loads(c):
            copy.start()

    below_v[...] = cx_ref[...]
    zadd = zadd_ref[gz]
    sub = lax.broadcasted_iota(jnp.int32, (SUB, LANES), 0)

    def scan(value, backward):
        def shifted(x, d):
            if backward:
                return jnp.where(sub < SUB - d, pltpu.roll(x, SUB - d, 0), 0.0)
            return jnp.where(sub >= d, pltpu.roll(x, d, 0), 0.0)

        for d in (1, 2, 4):
            value = value + shifted(value, d)
        return shifted(value, 1)

    def step(c, carry):
        for copy in loads(c):
            copy.wait()
        base = pl.multiple_of(c * PLANES, PLANES)
        wx = [[xtab_ref[kind, gx * east + base + p] for p in range(PLANES)] for kind in range(2)]
        add = []
        for p in range(PLANES):
            cz = cz_ref[base + p].T.astype(BF16)
            add.append(jnp.dot(cz, zadd, preferred_element_type=F32))
        for l in range(tiles):
            col = slice(l * LANES, (l + 1) * LANES)
            edge = [cy_ref[kind, pl.ds(base, PLANES), col] for kind in range(2)]
            low, high = [], []
            for p in range(PLANES):
                su, sv = sg_ref[0, base + p, :, col], sg_ref[1, base + p, :, col]
                low.append(scan(su, False) + edge[0][p:p + 1])
                high.append(scan(sv, True) + edge[1][p:p + 1] + sv)
            for t in range(steps):
                row = slice(t * SUB, (t + 1) * SUB)
                wu, wv = ytab_ref[gy, 0, row], ytab_ref[gy, 1, row]
                below, above = below_v[0, row, col], below_v[1, row, col]
                for p in range(PLANES):
                    i = base + p
                    g = g_v[l, i, row]
                    low[p] = low[p] + wu * g
                    high[p] = high[p] - wv * g
                    h = wv * low[p] + wu * high[p]
                    below = below + wx[0][p] * h
                    above = above - wx[1][p] * h
                    own = u_v[l, i, pl.ds(t, SUB, stride=steps), :]
                    o_v[l, i, pl.ds(t, SUB, stride=steps), :] = (
                        own + add[p][row, col] + (wx[1][p] * below + wx[0][p] * above))
                below_v[0, row, col] = below
                below_v[1, row, col] = above
        for copy in stores(c):
            copy.start()
        return carry

    lax.fori_loop(0, chunks, step, 0)
    for c in range(chunks):
        for copy in stores(c):
            copy.wait()


def final_pass(g, u, sg, cz, cy, cx, tables):
    east, north, upward = u.shape
    tiles = upward // LANES
    chunks = east // PLANES
    vmem = pl.BlockSpec(memory_space=pltpu.VMEM)
    smem = pl.BlockSpec(memory_space=pltpu.SMEM)
    hbm = pl.BlockSpec(memory_space=pl.ANY)
    block = pltpu.VMEM((tiles, east, north, LANES), F32)
    return pl.pallas_call(
        functools.partial(final_kernel, u.shape),
        name="final",
        out_shape=jax.ShapeDtypeStruct(u.shape, F32),
        in_specs=[hbm, hbm, vmem, vmem, vmem, vmem, vmem, vmem, smem],
        out_specs=hbm,
        scratch_shapes=[
            pltpu.VMEM((2, north, upward), F32),
            block, block, block,
            pltpu.SemaphoreType.DMA((tiles, chunks)),
            pltpu.SemaphoreType.DMA((tiles, chunks)),
            pltpu.SemaphoreType.DMA((tiles, chunks)),
        ],
    )(g, u, sg, cz, cy, cx, tables["zadd"], tables["y"], tables["x"])


def local(sizes, u, s):
    tables = make_tables(u.shape, sizes)
    g, sg, cz, cy, cx = local_pass(u, s, tables, sizes)
    return final_pass(g, u, sg, cz, cy, cx, tables)


def solution(mesh):
    sizes = tuple(mesh.shape[name] for name in ("gx", "gy", "gz"))
    spec = P("gx", "gy", "gz")
    return jax.shard_map(
        functools.partial(local, sizes), mesh=mesh, in_specs=(spec, spec), out_specs=spec, check_vma=False
    )
```

```python
import functools

import jax
import jax.numpy as jnp
import numpy as np
from jax import lax
from jax.experimental import pallas as pl
from jax.experimental.pallas import tpu as pltpu
from jax.sharding import PartitionSpec as P

MESH = pl.DeviceIdType.MESH
HIGH = lax.Precision.HIGHEST
F32 = jnp.float32
BF16 = jnp.bfloat16
LANES = 128
SUB = 8


def generators(whole, factor):
    half = 0.5 * factor
    theta = np.arccosh(1.0 + 0.5 / half)
    scale = np.sqrt(1.0 / (half * np.sinh(theta) * np.sinh((whole + 1) * theta)))
    index = np.arange(whole, dtype=np.float64)
    return np.sinh((index + 1) * theta) * scale, np.sinh((whole - index) * theta) * scale


def diagonal_blocks(u, v, members):
    extent = u.shape[0] // members
    blocks = []
    for member in range(members):
        part = slice(member * extent, (member + 1) * extent)
        own_u, own_v = u[part], v[part]
        lower = np.outer(own_v, own_u)
        blocks.append(np.where(np.tri(extent, dtype=bool), lower, lower.T))
    return np.stack(blocks)


def split_bf16(values):
    high = values.astype(np.float32).astype(BF16)
    low = (values - high.astype(np.float64)).astype(np.float32).astype(BF16)
    return np.asarray(high), np.asarray(low)


def split(values):
    high = values.astype(BF16)
    return high, (values - high.astype(F32)).astype(BF16)


def make_tables(shape, members):
    east, north, upward = shape
    wholes = [extent * count for extent, count in zip(shape, members)]
    factors = [float(whole * whole // 4) for whole in wholes]
    order = np.arange(north)
    order = (north // SUB) * (order % SUB) + order // SUB

    ux, vx = generators(wholes[0], factors[0])
    uy, vy = generators(wholes[1], factors[1])
    uz, vz = generators(wholes[2], factors[2])
    tables = {"factors": factors}
    tables["x"] = np.stack([ux, vx]).astype(np.float32)

    own = np.stack([w.reshape(members[1], north)[:, order] for w in (uy, vy)], 1)
    tables["y"] = np.repeat(own[..., None], LANES, -1).astype(np.float32)
    by = diagonal_blocks(uy, vy, members[1])[:, order][:, :, order]
    tables["by"] = by.astype(np.float32)
    tables["bx"] = diagonal_blocks(ux, vx, members[0]).astype(np.float32)
    yw = np.zeros((members[1], 2, 2, SUB, north), np.float32)
    xw = np.zeros((members[0], 2, 2, SUB, east), np.float32)
    for slot in range(2):
        yw[:, :, slot, slot] = own
        for kind, w in enumerate((ux, vx)):
            xw[:, kind, slot, slot] = w.reshape(members[0], east)
    tables["yw"], tables["xw"] = yw, xw
    wy = np.zeros((members[1], SUB, north), np.float32)
    wy[:, 0] = own[:, 1]
    wy[:, 1] = own[:, 0]
    tables["wy"] = wy

    bzh, bzl = split_bf16(diagonal_blocks(uz, vz, members[2]))
    tables["bz"] = np.stack([bzh, bzl], 1)
    zu, zv = uz.reshape(members[2], upward), vz.reshape(members[2], upward)
    uh, ul = split_bf16(zu)
    vh, vl = split_bf16(zv)
    zero = np.zeros_like(uh)
    tables["zmom"] = np.stack([uh, ul, vh, vl] + [zero] * 12, 1)
    tables["zadd"] = np.stack([vh, vh, vl, uh, uh, ul, zero, zero], 1)
    return tables


def at(axis, index):
    return {axis: index}


def greet(partners):
    barrier = pltpu.get_barrier_semaphore()
    for partner in partners:
        pl.semaphore_signal(barrier, inc=1, device_id=partner, device_id_type=MESH)
    pl.semaphore_wait(barrier, len(partners))


def remote(src, dst, send, recv, partner):
    return pltpu.make_async_remote_copy(
        src_ref=src, dst_ref=dst, send_sem=send, recv_sem=recv, device_id=partner, device_id_type=MESH
    )


def kind_to(me, count, o):
    return jnp.where(lax.rem(me + o, count) > me, 0, 1)


def gather(me, count, buf):
    left = right = None
    for o in range(1, count):
        low = jnp.where(lax.rem(me + count - o, count) < me, 1.0, 0.0).astype(F32)
        piece = buf[o - 1]
        left = piece * low if left is None else left + piece * low
        right = piece * (1.0 - low) if right is None else right + piece * (1.0 - low)
    return left, right


NN = (((1,), (0,)), ((), ()))
NT = (((1,), (1,)), ((), ()))
TN = (((0,), (0,)), ((), ()))


def dot(a, b, dims=NN):
    if dims == TN:
        return lax.dot_general(a, b, dims, precision=HIGH, preferred_element_type=F32)
    ah, al = split(a)
    bh, bl = split(b)
    left = jnp.concatenate([ah, al, ah], 1)
    right = jnp.concatenate([bl, bh, bh], dims[0][1][0])
    return lax.dot_general(left, right, dims, preferred_element_type=F32)


PLANES = 8
LOAD = 16


def stack_rows(rows, width=LANES):
    sub = lax.broadcasted_iota(jnp.int32, (SUB, width), 0)
    out = jnp.zeros((SUB, width), F32)
    for p, row in enumerate(rows):
        out = jnp.where(sub == p, row, out)
    return out


def local_kernel(
    sizes, shape, factors,
    u_ref, s_ref, bz_hbm, zmom_hbm, ytab_hbm, yw_hbm, xw_hbm, wy_hbm, by_hbm, bx_hbm, zadd_hbm, xtab_ref,
    g_v, u_v, sg_ref, cz_ref, cy_ref, cx_ref, ytab_ref, zadd_ref,
    bz_ref, zmom_ref, yw_ref, xw_ref, wy_ref, by_ref, bx_ref, tsem,
    s_v, fh0, fl0, fh1, fl1, y0, y1, hy, mxf, mxu, mx, my, mz,
    zbuf, zpad, ybuf, xpair, xtot, xbuf, xback, eown, ebuf, qown, qbuf, rown, rbuf, town, tbuf,
    usem, ssem, hs, hr, zs, zr, ys, yr, ps, pr, xs, xr, bs, br, es, er, qs, qr, rs, rr, ts, tr,
):
    gx, gy, gz = lax.axis_index("gx"), lax.axis_index("gy"), lax.axis_index("gz")
    nx, ny, nz = sizes
    east, north, upward = shape
    tiles = upward // LANES
    steps = north // SUB
    chunks = east // PLANES
    pairs = chunks // 2
    blocks = east // LOAD
    rx, ry, _ = factors
    chips = nx // 2
    half = north // 2
    chip, core = gx // 2, lax.rem(gx, 2)
    mine = pl.ds(pl.multiple_of(core * half, half), half)
    theirs = pl.ds(pl.multiple_of((1 - core) * half, half), half)
    partner = at("gx", chip * 2 + 1 - core)

    def u_loads(b):
        rows = pl.ds(b * LOAD, LOAD)
        return [
            pltpu.make_async_copy(
                u_ref.at[rows, pl.ds(k * steps, steps), :], u_v.at[pl.ds(1 + b * LOAD, LOAD), :, k, :],
                usem.at[b, k])
            for k in range(SUB)
        ]

    def s_loads(b):
        rows = pl.ds(b * LOAD, LOAD)
        return [
            pltpu.make_async_copy(
                s_ref.at[rows, pl.ds(k * steps, steps), :], s_v.at[rows, :, k, :], ssem.at[b, k])
            for k in range(SUB)
        ]

    early = sorted({0, blocks - 1})
    for b in early + [b for b in range(blocks) if b not in early]:
        for copy in u_loads(b):
            copy.start()
    for b in range(blocks):
        for copy in s_loads(b):
            copy.start()

    table_loads = [
        pltpu.make_async_copy(hbm.at[index], ref, tsem.at[n])
        for n, (hbm, index, ref) in enumerate((
            (bz_hbm, gz, bz_ref), (zmom_hbm, gz, zmom_ref), (ytab_hbm, gy, ytab_ref), (yw_hbm, gy, yw_ref),
            (xw_hbm, gx, xw_ref), (wy_hbm, gy, wy_ref), (by_hbm, gy, by_ref), (bx_hbm, gx, bx_ref),
            (zadd_hbm, gz, zadd_ref)))
    ]
    for copy in table_loads:
        copy.start()

    def ring(axis, me, count):
        return [at(axis, lax.rem(me + o, count)) for o in range(1, count)]

    greet(ring("gx", gx, nx) + ring("gy", gy, ny) + ring("gz", gz, nz))

    xr_, xl_ = lax.rem(gx + 1, nx), lax.rem(gx + nx - 1, nx)
    yr_, yl_ = lax.rem(gy + 1, ny), lax.rem(gy + ny - 1, ny)
    halos = [
        remote(u_ref.at[:, north - 1, :], hy.at[0], hs.at[2], hr.at[2], at("gy", yr_)),
        remote(u_ref.at[:, 0, :], hy.at[1], hs.at[3], hr.at[3], at("gy", yl_)),
        remote(u_v.at[east], u_v.at[0], hs.at[0], hr.at[0], at("gx", xr_)),
        remote(u_v.at[1], u_v.at[east + 1], hs.at[1], hr.at[1], at("gx", xl_)),
    ]
    for copy in halos[:2]:
        copy.start()
    for b in early:
        for copy in u_loads(b):
            copy.wait()
    for copy in halos[2:]:
        copy.start()

    sub = lax.broadcasted_iota(jnp.int32, (SUB, LANES), 0)

    def cols(l):
        return slice(l * LANES, (l + 1) * LANES)

    def rows_at(t):
        return slice(t * SUB, (t + 1) * SUB)

    mxu[...] = jnp.zeros_like(mxu)
    mxf[...] = jnp.zeros_like(mxf)
    zpad[...] = jnp.zeros_like(zpad)

    def weights(base):
        return [[xtab_ref[kind, gx * east + base + p] for p in range(PLANES)] for kind in range(2)]

    def pre(c, carry):
        block = c * PLANES // LOAD
        waits = lax.rem(c * PLANES, LOAD) == 0
        for b in early:
            waits = jnp.logical_and(waits, block != b)

        @pl.when(waits)
        def _():
            for copy in u_loads(block):
                copy.wait()

        base = c * PLANES
        w = weights(base)
        for l in range(tiles):
            for t in range(steps):
                acc = [mxu[kind, rows_at(t), cols(l)] for kind in range(2)]
                for p in range(PLANES):
                    own = u_v[base + p + 1, t, :, cols(l)]
                    for kind in range(2):
                        acc[kind] = acc[kind] + w[kind][p] * own
                for kind in range(2):
                    mxu[kind, rows_at(t), cols(l)] = acc[kind]
        return carry

    lax.fori_loop(0, chunks, pre, 0)

    for copy in halos:
        copy.wait()
    before = jnp.where(gx > 0, 1.0, 0.0).astype(F32)
    after = jnp.where(gx < nx - 1, 1.0, 0.0).astype(F32)
    south = jnp.where(gy > 0, 1.0, 0.0).astype(F32)
    nord = jnp.where(gy < ny - 1, 1.0, 0.0).astype(F32)
    u_v[0] = u_v[0] * before
    u_v[east + 1] = u_v[east + 1] * after

    for copy in table_loads:
        copy.wait()
    zmom = zmom_ref[...]
    halves = ((fh0, fl0), (fh1, fl1))

    def z_moments(source, k, c):
        mom = None
        for f in source:
            flat = f[k].reshape(PLANES * north, upward)
            part = lax.dot_general(zmom, flat, NT, preferred_element_type=F32)
            mom = part if mom is None else mom + part
        for kind in range(2):
            m = mom[2 * kind:2 * kind + 1] + mom[2 * kind + 1:2 * kind + 2]
            mz[kind, pl.ds(pl.multiple_of(c * PLANES, PLANES), PLANES), :] = stack_rows(
                [m[:, p * north:(p + 1) * north] for p in range(PLANES)])

    def rhs(target, k, c):
        high_ref, low_ref = target
        base = pl.multiple_of(c * PLANES, PLANES)
        w = weights(base)
        for l in range(tiles):
            col = cols(l)
            edge = [hy[0, pl.ds(base, PLANES), col] * south, hy[1, pl.ds(base, PLANES), col] * nord]
            for t2 in range(0, steps, 2):
                acc = [[mxf[kind, rows_at(t2 + j), col] for j in range(2)] for kind in range(2)]
                column = [[u_v[base + p, t2 + j, :, col] for p in range(PLANES + 2)] for j in range(2)]
                for p in range(PLANES):
                    i = base + p
                    if t2 == 0:
                        below = pltpu.roll(u_v[i + 1, steps - 1, :, col], 1, 0)
                        below = jnp.where(sub == 0, edge[0][p:p + 1], below)
                    else:
                        below = u_v[i + 1, t2 - 1, :, col]
                    if t2 == steps - 2:
                        above = pltpu.roll(u_v[i + 1, 0, :, col], SUB - 1, 0)
                        above = jnp.where(sub == SUB - 1, edge[1][p:p + 1], above)
                    else:
                        above = u_v[i + 1, t2 + 2, :, col]
                    out = []
                    for j in range(2):
                        own = column[j][p + 1]
                        across = column[j][p] + column[j][p + 2]
                        along = (below + column[1][p + 1]) if j == 0 else (column[0][p + 1] + above)
                        if rx == ry:
                            spread = rx * ((across + along) + (2.0 / rx - 4.0) * own)
                        else:
                            spread = rx * across + ry * along + (2.0 - 2.0 * rx - 2.0 * ry) * own
                        f = s_v[i, t2 + j, :, col] + spread
                        for kind in range(2):
                            acc[kind][j] = acc[kind][j] + w[kind][p] * f
                        out.append(f)
                    pair = jnp.concatenate(out, 0)
                    high = pair.astype(BF16)
                    rows = slice(t2 * SUB, (t2 + 2) * SUB)
                    high_ref[k, p, rows, col] = high
                    low_ref[k, p, rows, col] = (pair - high.astype(F32)).astype(BF16)
                for kind in range(2):
                    for j in range(2):
                        mxf[kind, rows_at(t2 + j), col] = acc[kind][j]

    def rhs_pair(k, carry):
        waits = lax.rem(k * 2 * PLANES, LOAD) == 0

        @pl.when(waits)
        def _():
            for copy in s_loads(k * 2 * PLANES // LOAD):
                copy.wait()

        late = jnp.maximum(k - 1, 0)
        z_moments(halves[1], late, 2 * late + 1)
        rhs(halves[0], k, 2 * k)
        z_moments(halves[0], k, 2 * k)
        rhs(halves[1], k, 2 * k + 1)
        return carry

    lax.fori_loop(0, pairs, rhs_pair, 0)
    z_moments(halves[1], pairs - 1, chunks - 1)

    zcopies = [
        remote(mz.at[kind_to(gz, nz, o)], zbuf.at[o - 1], zs.at[o - 1], zr.at[o - 1],
               at("gz", lax.rem(gz + o, nz)))
        for o in range(1, nz)
    ]
    for copy in zcopies:
        copy.start()

    def solve_up(high, low):
        stack = jnp.concatenate([bz_ref[1], bz_ref[0], bz_ref[0]], 0)
        return jnp.dot(jnp.concatenate([high, low, high], 1), stack, preferred_element_type=F32)

    fold_h, fold_l = split(mxf[...].reshape(2 * north, upward))
    mx[...] = solve_up(fold_h, fold_l).reshape(2, north, upward) - 2.0 * mxu[...]

    pair = remote(mx.at[:, theirs, :], xpair, ps, pr, partner)
    pair.start()
    for kind in range(2):
        qown[kind] = dot(yw_ref[kind, 0], mx[0]) + dot(yw_ref[kind, 1], mx[1])
    qcopies = [
        remote(qown.at[kind_to(gy, ny, o)], qbuf.at[o - 1], qs.at[o - 1], qr.at[o - 1],
               at("gy", lax.rem(gy + o, ny)))
        for o in range(1, ny)
    ]
    for copy in qcopies:
        copy.start()
    xcopies = [
        remote(xtot.at[kind_to(chip, chips, o)], xbuf.at[o - 1], xs.at[o - 1], xr.at[o - 1],
               at("gx", lax.rem(chip + o, chips) * 2 + core))
        for o in range(1, chips)
    ]
    rcopies = [
        remote(rown.at[kind_to(gx, nx, o)], rbuf.at[o - 1], rs.at[o - 1], rr.at[o - 1],
               at("gx", lax.rem(gx + o, nx)))
        for o in range(1, nx)
    ]

    def send_chips():
        pair.wait()
        xtot[0] = mx[0, mine, :] + xpair[0]
        xtot[1] = mx[1, mine, :] + xpair[1]
        for copy in xcopies:
            copy.start()

    def send_edges():
        for copy in qcopies:
            copy.wait()
        qleft, qright = gather(gy, ny, qbuf)
        for kind in range(2):
            rown[kind] = stack_rows([qleft[kind:kind + 1], qright[kind:kind + 1]], upward)
        for copy in rcopies:
            copy.start()

    def multiply(source, k, target):
        high_ref, low_ref = source
        target[...] = solve_up(
            high_ref[k].reshape(PLANES * north, upward), low_ref[k].reshape(PLANES * north, upward))

    def finish(source, c):
        base = pl.multiple_of(c * PLANES, PLANES)
        for l in range(tiles):
            col = cols(l)
            sums = [[None] * PLANES for _ in range(2)]
            for t in range(steps):
                w = [ytab_ref[kind, rows_at(t)] for kind in range(2)]
                for p in range(PLANES):
                    i = base + p
                    own = u_v[i + 1, t, :, col]
                    g = source[p * north + t * SUB:p * north + (t + 1) * SUB, col] - 2.0 * own
                    g_v[i, t, :, col] = g
                    for kind in range(2):
                        term = w[kind] * g
                        sums[kind][p] = term if t == 0 else sums[kind][p] + term
            for kind in range(2):
                for p in range(PLANES):
                    sg_ref[kind, base + p, :, col] = sums[kind][p]
                my[kind, pl.ds(base, PLANES), col] = stack_rows(
                    [jnp.sum(sums[kind][p], 0, keepdims=True) for p in range(PLANES)])

    def solve_pair(k, carry):
        @pl.when(k == min(1, pairs - 1))
        def _():
            send_chips()

        @pl.when(k == pairs - 1)
        def _():
            send_edges()

        multiply(halves[0], k, y0)
        finish(y1, jnp.maximum(2 * k - 1, 0))
        multiply(halves[1], k, y1)
        finish(y0, 2 * k)
        return carry

    lax.fori_loop(0, pairs, solve_pair, 0)
    finish(y1, chunks - 1)

    for copy in zcopies:
        copy.wait()
    coef = gather(gz, nz, zbuf)
    for m in range(2):
        zpad[m, 0:east] = coef[m]
    for kind in range(2):
        eown[kind] = dot(yw_ref[kind, 0], zpad[0], NT) + dot(yw_ref[kind, 1], zpad[1], NT)
    ecopies = [
        remote(eown.at[kind_to(gy, ny, o)], ebuf.at[o - 1], es.at[o - 1], er.at[o - 1],
               at("gy", lax.rem(gy + o, ny)))
        for o in range(1, ny)
    ]
    for copy in ecopies:
        copy.start()
    ycopies = [
        remote(my.at[kind_to(gy, ny, o)], ybuf.at[o - 1], ys.at[o - 1], yr.at[o - 1],
               at("gy", lax.rem(gy + o, ny)))
        for o in range(1, ny)
    ]
    for copy in ycopies:
        copy.start()

    by = by_ref[...]
    face = [dot(coef[m], by) for m in range(2)]
    for copy in ecopies:
        copy.wait()
    eleft, eright = gather(gy, ny, ebuf)
    for m in range(2):
        face[m] = face[m] + (
            dot(eleft, yw_ref[1, m], TN) + dot(eright, yw_ref[0, m], TN))[0:east]
    for kind in range(2):
        town[kind] = dot(xw_ref[kind, 0], face[0]) + dot(xw_ref[kind, 1], face[1])
    tcopies = [
        remote(town.at[kind_to(gx, nx, o)], tbuf.at[o - 1], ts.at[o - 1], tr.at[o - 1],
               at("gx", lax.rem(gx + o, nx)))
        for o in range(1, nx)
    ]
    for copy in tcopies:
        copy.start()
    bx = bx_ref[...]
    face = [dot(bx, face[m]) for m in range(2)]

    for copy in xcopies:
        copy.wait()
    px, sx = gather(chip, chips, xbuf)
    first = jnp.where(core == 0, 1.0, 0.0).astype(F32)
    second = 1.0 - first
    xback[0] = px + first * mx[0, mine, :]
    xback[1] = sx + second * mx[1, mine, :]
    back = remote(xback, cx_ref.at[:, mine, :], bs, br, partner)
    back.start()
    cx_ref[0, mine, :] = px + second * xpair[0]
    cx_ref[1, mine, :] = sx + first * xpair[1]
    for copy in rcopies:
        copy.wait()
    rleft, rright = gather(gx, nx, rbuf)
    rright = rright + rown[1]
    back.wait()
    wy = wy_ref[...]
    cx_ref[0] = dot(by, cx_ref[0]) + dot(wy, rleft, TN)
    cx_ref[1] = dot(by, cx_ref[1] + mx[1]) + dot(wy, rright, TN)

    for copy in tcopies:
        copy.wait()
    tleft, tright = gather(gx, nx, tbuf)
    for m in range(2):
        value = face[m] + dot(xw_ref[1, m], tleft, TN) + dot(xw_ref[0, m], tright, TN)
        high = value.astype(BF16).astype(F32)
        cz_ref[:, 3 * m, :] = high
        cz_ref[:, 3 * m + 1, :] = (value - high).astype(BF16).astype(F32)
        cz_ref[:, 3 * m + 2, :] = high
        cz_ref[:, 6 + m, :] = jnp.zeros_like(value)

    for copy in ycopies:
        copy.wait()
    left, right = gather(gy, ny, ybuf)
    cy_ref[0] = left
    cy_ref[1] = right


def local_pass(u, s, tables, sizes):
    east, north, upward = u.shape
    nx, ny, nz = sizes
    steps = north // SUB
    pairs = east // (2 * PLANES)
    blocks = east // LOAD
    chips = nx // 2
    half = north // 2
    vmem = pl.BlockSpec(memory_space=pltpu.VMEM)
    smem = pl.BlockSpec(memory_space=pltpu.SMEM)
    hbm = pl.BlockSpec(memory_space=pltpu.HBM)
    dma = pltpu.SemaphoreType.DMA

    def buf(*dims):
        return pltpu.VMEM(dims, F32)

    def halves():
        return pltpu.VMEM((pairs, PLANES, north, upward), BF16)

    names = ("bz", "zmom", "y", "yw", "xw", "wy", "by", "bx", "zadd")
    return pl.pallas_call(
        functools.partial(local_kernel, sizes, u.shape, tables["factors"]),
        name="local",
        out_shape=(
            buf(east, steps, SUB, upward),
            buf(east + 2, steps, SUB, upward),
            buf(2, east, SUB, upward),
            buf(east, SUB, north),
            buf(2, east, upward),
            buf(2, north, upward),
            buf(2, north, LANES),
            pltpu.VMEM((SUB, upward), BF16),
        ),
        in_specs=[hbm, hbm] + [hbm] * len(names) + [smem],
        out_specs=(vmem,) * 8,
        scratch_shapes=[
            pltpu.VMEM((2, upward, upward), BF16), pltpu.VMEM((16, upward), BF16),
            buf(2, 2, SUB, north), buf(2, 2, SUB, east), buf(SUB, north), buf(north, north), buf(east, east),
            dma((len(names),)),
            buf(east, steps, SUB, upward),
            halves(), halves(), halves(), halves(),
            buf(PLANES * north, upward), buf(PLANES * north, upward),
            buf(2, east, upward),
            buf(2, north, upward), buf(2, north, upward), buf(2, north, upward),
            buf(2, east, upward), buf(2, east, north),
            buf(nz - 1, east, north), buf(2, LANES, north), buf(ny - 1, east, upward),
            buf(2, half, upward), buf(2, half, upward), buf(chips - 1, half, upward), buf(2, half, upward),
            buf(2, SUB, LANES), buf(ny - 1, SUB, LANES),
            buf(2, SUB, upward), buf(ny - 1, SUB, upward),
            buf(2, SUB, upward), buf(nx - 1, SUB, upward),
            buf(2, SUB, north), buf(nx - 1, SUB, north),
            dma((blocks, SUB)), dma((blocks, SUB)),
            dma((4,)), dma((4,)),
            dma((nz - 1,)), dma((nz - 1,)),
            dma((ny - 1,)), dma((ny - 1,)),
            dma, dma,
            dma((chips - 1,)), dma((chips - 1,)),
            dma, dma,
            dma((ny - 1,)), dma((ny - 1,)),
            dma((ny - 1,)), dma((ny - 1,)),
            dma((nx - 1,)), dma((nx - 1,)),
            dma((nx - 1,)), dma((nx - 1,)),
        ],
        compiler_params=pltpu.CompilerParams(
            collective_id=0, has_side_effects=True, vmem_limit_bytes=LOCAL_VMEM),
    )(*[pltpu.with_memory_space_constraint(a, pltpu.HBM) for a in [u, s] + [tables[name] for name in names + ("x",)]])


LOCAL_VMEM = 34 * 2**20
FINAL_VMEM = 24 * 2**20


def final_kernel(
    shape,
    g_v, u_v, sg_ref, cz_ref, cy_ref, cx_ref, zadd_ref, ytab_ref, xtab_ref,
    o_ref,
    edge_v, o_v, osem,
):
    gx, gy, gz = lax.axis_index("gx"), lax.axis_index("gy"), lax.axis_index("gz")
    east, north, upward = shape
    tiles = upward // LANES
    steps = north // SUB
    chunks = east // PLANES

    def stores(c):
        rows = pl.ds(c * PLANES, PLANES)
        return [
            pltpu.make_async_copy(
                o_v.at[rows, :, k, :], o_ref.at[rows, pl.ds(k * steps, steps), :], osem.at[c, k])
            for k in range(SUB)
        ]

    edge_v[...] = cx_ref[...]
    zadd = zadd_ref[...]
    sub = lax.broadcasted_iota(jnp.int32, (SUB, LANES), 0)

    def scan(value, backward):
        def shifted(x, d):
            if backward:
                return jnp.where(sub < SUB - d, pltpu.roll(x, SUB - d, 0), 0.0)
            return jnp.where(sub >= d, pltpu.roll(x, d, 0), 0.0)

        for d in (1, 2, 4):
            value = value + shifted(value, d)
        return shifted(value, 1)

    def step(c, carry):
        base = pl.multiple_of(c * PLANES, PLANES)
        wx = [[xtab_ref[kind, gx * east + base + p] for p in range(PLANES)] for kind in range(2)]
        add = []
        for p in range(PLANES):
            cz = cz_ref[base + p].T.astype(BF16)
            add.append(jnp.dot(cz, zadd, preferred_element_type=F32))
        for l in range(tiles):
            col = slice(l * LANES, (l + 1) * LANES)
            edge = [cy_ref[kind, pl.ds(base, PLANES), col] for kind in range(2)]
            low, high = [], []
            for p in range(PLANES):
                su, sv = sg_ref[0, base + p, :, col], sg_ref[1, base + p, :, col]
                low.append(scan(su, False) + edge[0][p:p + 1])
                high.append(scan(sv, True) + edge[1][p:p + 1] + sv)
            for t in range(steps):
                row = slice(t * SUB, (t + 1) * SUB)
                wu, wv = ytab_ref[0, row], ytab_ref[1, row]
                below, above = edge_v[0, row, col], edge_v[1, row, col]
                for p in range(PLANES):
                    i = base + p
                    g = g_v[i, t, :, col]
                    low[p] = low[p] + wu * g
                    high[p] = high[p] - wv * g
                    h = wv * low[p] + wu * high[p]
                    below = below + wx[0][p] * h
                    above = above - wx[1][p] * h
                    o_v[i, t, :, col] = (
                        u_v[i + 1, t, :, col] + add[p][row, col] + (wx[1][p] * below + wx[0][p] * above))
                edge_v[0, row, col] = below
                edge_v[1, row, col] = above
        for copy in stores(c):
            copy.start()
        return carry

    lax.fori_loop(0, chunks, step, 0)
    for c in range(chunks):
        for copy in stores(c):
            copy.wait()


def final_pass(g, u, sg, cz, cy, cx, ytab, zadd, tables, shape):
    east, north, upward = shape
    steps = north // SUB
    chunks = east // PLANES
    vmem = pl.BlockSpec(memory_space=pltpu.VMEM)
    smem = pl.BlockSpec(memory_space=pltpu.SMEM)
    return pl.pallas_call(
        functools.partial(final_kernel, shape),
        name="final",
        out_shape=jax.ShapeDtypeStruct(shape, F32),
        in_specs=[vmem] * 8 + [smem],
        out_specs=pl.BlockSpec(memory_space=pl.ANY),
        scratch_shapes=[
            pltpu.VMEM((2, north, upward), F32),
            pltpu.VMEM((east, steps, SUB, upward), F32),
            pltpu.SemaphoreType.DMA((chunks, SUB)),
        ],
        compiler_params=pltpu.CompilerParams(vmem_limit_bytes=FINAL_VMEM),
    )(g, u, sg, cz, cy, cx, zadd, ytab, tables["x"])


def local(sizes, u, s):
    tables = make_tables(u.shape, sizes)
    g, padded, *faces = local_pass(u, s, tables, sizes)
    return final_pass(g, padded, *faces, tables, u.shape)


def solution(mesh):
    sizes = tuple(mesh.shape[name] for name in ("gx", "gy", "gz"))
    spec = P("gx", "gy", "gz")
    return jax.shard_map(
        functools.partial(local, sizes), mesh=mesh, in_specs=(spec, spec), out_specs=spec, check_vma=False
    )
```

```python
import functools

import jax
import jax.numpy as jnp
import numpy as np
from jax import lax
from jax.experimental import pallas as pl
from jax.experimental.pallas import tpu as pltpu
from jax.sharding import PartitionSpec as P

MESH = pl.DeviceIdType.MESH
HIGH = lax.Precision.HIGHEST
F32 = jnp.float32
BF16 = jnp.bfloat16
LANES = 128
SUB = 8


def generators(whole, factor):
    half = 0.5 * factor
    theta = np.arccosh(1.0 + 0.5 / half)
    scale = np.sqrt(1.0 / (half * np.sinh(theta) * np.sinh((whole + 1) * theta)))
    index = np.arange(whole, dtype=np.float64)
    return np.sinh((index + 1) * theta) * scale, np.sinh((whole - index) * theta) * scale


def diagonal_blocks(u, v, members):
    extent = u.shape[0] // members
    blocks = []
    for member in range(members):
        part = slice(member * extent, (member + 1) * extent)
        own_u, own_v = u[part], v[part]
        lower = np.outer(own_v, own_u)
        blocks.append(np.where(np.tri(extent, dtype=bool), lower, lower.T))
    return np.stack(blocks)


def split_bf16(values):
    high = values.astype(np.float32).astype(BF16)
    low = (values - high.astype(np.float64)).astype(np.float32).astype(BF16)
    return np.asarray(high), np.asarray(low)


def split(values):
    high = values.astype(BF16)
    return high, (values - high.astype(F32)).astype(BF16)


def make_tables(shape, members):
    east, north, upward = shape
    wholes = [extent * count for extent, count in zip(shape, members)]
    factors = [float(whole * whole // 4) for whole in wholes]
    order = np.arange(north)
    order = (north // SUB) * (order % SUB) + order // SUB

    ux, vx = generators(wholes[0], factors[0])
    uy, vy = generators(wholes[1], factors[1])
    uz, vz = generators(wholes[2], factors[2])
    tables = {"factors": factors}
    tables["x"] = np.stack([ux, vx]).astype(np.float32)

    own = np.stack([w.reshape(members[1], north)[:, order] for w in (uy, vy)], 1)
    tables["y"] = np.repeat(own[..., None], LANES, -1).astype(np.float32)
    by = diagonal_blocks(uy, vy, members[1])[:, order][:, :, order]
    tables["by"] = by.astype(np.float32)
    tables["bx"] = diagonal_blocks(ux, vx, members[0]).astype(np.float32)
    yw = np.zeros((members[1], 2, 2, SUB, north), np.float32)
    xw = np.zeros((members[0], 2, 2, SUB, east), np.float32)
    for slot in range(2):
        yw[:, :, slot, slot] = own
        for kind, w in enumerate((ux, vx)):
            xw[:, kind, slot, slot] = w.reshape(members[0], east)
    tables["yw"], tables["xw"] = yw, xw
    wy = np.zeros((members[1], SUB, north), np.float32)
    wy[:, 0] = own[:, 1]
    wy[:, 1] = own[:, 0]
    tables["wy"] = wy

    bzh, bzl = split_bf16(diagonal_blocks(uz, vz, members[2]))
    tables["bz"] = np.stack([bzh, bzl], 1)
    zu, zv = uz.reshape(members[2], upward), vz.reshape(members[2], upward)
    uh, ul = split_bf16(zu)
    vh, vl = split_bf16(zv)
    zero = np.zeros_like(uh)
    tables["zmom"] = np.stack([uh, ul, vh, vl] + [zero] * (LANES - 4), 2)
    tables["zadd"] = np.stack([vh, vh, vl, uh, uh, ul, zero, zero], 1)
    return tables


def at(axis, index):
    return {axis: index}


def greet(partners):
    barrier = pltpu.get_barrier_semaphore()
    for partner in partners:
        pl.semaphore_signal(barrier, inc=1, device_id=partner, device_id_type=MESH)
    pl.semaphore_wait(barrier, len(partners))


def remote(src, dst, send, recv, partner):
    return pltpu.make_async_remote_copy(
        src_ref=src, dst_ref=dst, send_sem=send, recv_sem=recv, device_id=partner, device_id_type=MESH
    )


def kind_to(me, count, o):
    return jnp.where(lax.rem(me + o, count) > me, 0, 1)


def gather(me, count, buf):
    left = right = None
    for o in range(1, count):
        low = jnp.where(lax.rem(me + count - o, count) < me, 1.0, 0.0).astype(F32)
        piece = buf[o - 1]
        left = piece * low if left is None else left + piece * low
        right = piece * (1.0 - low) if right is None else right + piece * (1.0 - low)
    return left, right


NN = (((1,), (0,)), ((), ()))
NT = (((1,), (1,)), ((), ()))
TN = (((0,), (0,)), ((), ()))


def dot(a, b, dims=NN):
    if dims == TN:
        return lax.dot_general(a, b, dims, precision=HIGH, preferred_element_type=F32)
    ah, al = split(a)
    bh, bl = split(b)
    left = jnp.concatenate([ah, al, ah], 1)
    right = jnp.concatenate([bl, bh, bh], dims[0][1][0])
    return lax.dot_general(left, right, dims, preferred_element_type=F32)


PLANES = 8
LOAD = 16


def stack_rows(rows, width=LANES):
    sub = lax.broadcasted_iota(jnp.int32, (SUB, width), 0)
    out = jnp.zeros((SUB, width), F32)
    for p, row in enumerate(rows):
        out = jnp.where(sub == p, row, out)
    return out


def local_kernel(
    sizes, shape, factors,
    u_ref, s_ref, bz_hbm, zmom_hbm, ytab_hbm, yw_hbm, xw_hbm, wy_hbm, by_hbm, bx_hbm, zadd_hbm, xtab_ref,
    g_v, u_v, sg_ref, cz_ref, cy_ref, cx_ref, ytab_ref, zadd_ref,
    bz_ref, zmom_ref, yw_ref, xw_ref, wy_ref, by_ref, bx_ref, tsem,
    s_v, fh0, fl0, fh1, fl1, y0, y1, hy, mxf, mxu, mx, my, mz,
    zbuf, zpad, ybuf, xpair, xtot, xbuf, xback, eown, ebuf, qown, qbuf, rown, rbuf, town, tbuf, face,
    usem, ssem, hs, hr, zs, zr, ys, yr, ps, pr, xs, xr, bs, br, es, er, qs, qr, rs, rr, ts, tr,
):
    gx, gy, gz = lax.axis_index("gx"), lax.axis_index("gy"), lax.axis_index("gz")
    nx, ny, nz = sizes
    east, north, upward = shape
    tiles = upward // LANES
    steps = north // SUB
    chunks = east // PLANES
    pairs = chunks // 2
    blocks = east // LOAD
    rx, ry, _ = factors
    chips = nx // 2
    half = north // 2
    chip, core = gx // 2, lax.rem(gx, 2)
    mine = pl.ds(pl.multiple_of(core * half, half), half)
    theirs = pl.ds(pl.multiple_of((1 - core) * half, half), half)
    partner = at("gx", chip * 2 + 1 - core)

    def u_loads(b):
        rows = pl.ds(b * LOAD, LOAD)
        return [
            pltpu.make_async_copy(
                u_ref.at[rows, pl.ds(k * steps, steps), :], u_v.at[pl.ds(1 + b * LOAD, LOAD), :, k, :],
                usem.at[b, k])
            for k in range(SUB)
        ]

    def s_loads(b):
        rows = pl.ds(b * LOAD, LOAD)
        return [
            pltpu.make_async_copy(
                s_ref.at[rows, pl.ds(k * steps, steps), :], s_v.at[rows, :, k, :], ssem.at[b, k])
            for k in range(SUB)
        ]

    early = sorted({0, blocks - 1})
    for b in early + [b for b in range(blocks) if b not in early]:
        for copy in u_loads(b):
            copy.start()
    table_loads = [
        pltpu.make_async_copy(hbm.at[index], ref, tsem.at[n])
        for n, (hbm, index, ref) in enumerate((
            (bz_hbm, gz, bz_ref), (zmom_hbm, gz, zmom_ref), (ytab_hbm, gy, ytab_ref), (yw_hbm, gy, yw_ref),
            (xw_hbm, gx, xw_ref), (wy_hbm, gy, wy_ref), (by_hbm, gy, by_ref), (bx_hbm, gx, bx_ref),
            (zadd_hbm, gz, zadd_ref)))
    ]
    for copy in table_loads:
        copy.start()

    def ring(axis, me, count):
        return [at(axis, lax.rem(me + o, count)) for o in range(1, count)]

    greet(ring("gx", gx, nx) + ring("gy", gy, ny) + ring("gz", gz, nz))

    xr_, xl_ = lax.rem(gx + 1, nx), lax.rem(gx + nx - 1, nx)
    yr_, yl_ = lax.rem(gy + 1, ny), lax.rem(gy + ny - 1, ny)
    halos = [
        remote(u_ref.at[:, north - 1, :], hy.at[0], hs.at[2], hr.at[2], at("gy", yr_)),
        remote(u_ref.at[:, 0, :], hy.at[1], hs.at[3], hr.at[3], at("gy", yl_)),
        remote(u_v.at[east], u_v.at[0], hs.at[0], hr.at[0], at("gx", xr_)),
        remote(u_v.at[1], u_v.at[east + 1], hs.at[1], hr.at[1], at("gx", xl_)),
    ]
    for copy in halos[:2]:
        copy.start()
    for b in early:
        for copy in u_loads(b):
            copy.wait()
    for copy in halos[2:]:
        copy.start()
    for b in range(blocks):
        for copy in s_loads(b):
            copy.start()

    sub = lax.broadcasted_iota(jnp.int32, (SUB, LANES), 0)

    def cols(l):
        return slice(l * LANES, (l + 1) * LANES)

    def rows_at(t):
        return slice(t * SUB, (t + 1) * SUB)

    mxu[...] = jnp.zeros_like(mxu)
    mxf[...] = jnp.zeros_like(mxf)
    zpad[...] = jnp.zeros_like(zpad)

    def weights(base):
        return [[xtab_ref[kind, gx * east + base + p] for p in range(PLANES)] for kind in range(2)]

    def pre(c, carry):
        block = c * PLANES // LOAD
        waits = lax.rem(c * PLANES, LOAD) == 0
        for b in early:
            waits = jnp.logical_and(waits, block != b)

        @pl.when(waits)
        def _():
            for copy in u_loads(block):
                copy.wait()

        base = c * PLANES
        w = weights(base)
        for l in range(tiles):
            for t in range(steps):
                acc = [mxu[kind, rows_at(t), cols(l)] for kind in range(2)]
                for p in range(PLANES):
                    own = u_v[base + p + 1, t, :, cols(l)]
                    for kind in range(2):
                        acc[kind] = acc[kind] + w[kind][p] * own
                for kind in range(2):
                    mxu[kind, rows_at(t), cols(l)] = acc[kind]
        return carry

    lax.fori_loop(0, chunks, pre, 0)

    for copy in halos:
        copy.wait()
    before = jnp.where(gx > 0, 1.0, 0.0).astype(F32)
    after = jnp.where(gx < nx - 1, 1.0, 0.0).astype(F32)
    south = jnp.where(gy > 0, 1.0, 0.0).astype(F32)
    nord = jnp.where(gy < ny - 1, 1.0, 0.0).astype(F32)
    u_v[0] = u_v[0] * before
    u_v[east + 1] = u_v[east + 1] * after

    for copy in table_loads:
        copy.wait()
    zmom = zmom_ref[...]
    halves = ((fh0, fl0), (fh1, fl1))

    def z_moments(source, k, c):
        flat = jnp.concatenate([f[k].reshape(PLANES * north, upward) for f in source], 1)
        mom = jnp.dot(flat, jnp.concatenate([zmom, zmom], 0), preferred_element_type=F32)
        across = [mom[p * north:(p + 1) * north].T for p in range(PLANES)]
        for kind in range(2):
            mz[kind, pl.ds(pl.multiple_of(c * PLANES, PLANES), PLANES), :] = stack_rows(
                [a[2 * kind:2 * kind + 1] + a[2 * kind + 1:2 * kind + 2] for a in across])

    def rhs(target, k, c):
        high_ref, low_ref = target
        base = pl.multiple_of(c * PLANES, PLANES)
        w = weights(base)
        for l in range(tiles):
            col = cols(l)
            edge = [hy[0, pl.ds(base, PLANES), col] * south, hy[1, pl.ds(base, PLANES), col] * nord]
            for t2 in range(0, steps, 2):
                acc = [[mxf[kind, rows_at(t2 + j), col] for j in range(2)] for kind in range(2)]
                column = [[u_v[base + p, t2 + j, :, col] for p in range(PLANES + 2)] for j in range(2)]
                for p in range(PLANES):
                    i = base + p
                    if t2 == 0:
                        below = pltpu.roll(u_v[i + 1, steps - 1, :, col], 1, 0)
                        below = jnp.where(sub == 0, edge[0][p:p + 1], below)
                    else:
                        below = u_v[i + 1, t2 - 1, :, col]
                    if t2 == steps - 2:
                        above = pltpu.roll(u_v[i + 1, 0, :, col], SUB - 1, 0)
                        above = jnp.where(sub == SUB - 1, edge[1][p:p + 1], above)
                    else:
                        above = u_v[i + 1, t2 + 2, :, col]
                    out = []
                    for j in range(2):
                        own = column[j][p + 1]
                        across = column[j][p] + column[j][p + 2]
                        along = (below + column[1][p + 1]) if j == 0 else (column[0][p + 1] + above)
                        if rx == ry:
                            spread = rx * ((across + along) + (2.0 / rx - 4.0) * own)
                        else:
                            spread = rx * across + ry * along + (2.0 - 2.0 * rx - 2.0 * ry) * own
                        f = s_v[i, t2 + j, :, col] + spread
                        for kind in range(2):
                            acc[kind][j] = acc[kind][j] + w[kind][p] * f
                        out.append(f)
                    pair = jnp.concatenate(out, 0)
                    high = pair.astype(BF16)
                    rows = slice(t2 * SUB, (t2 + 2) * SUB)
                    high_ref[k, p, rows, col] = high
                    low_ref[k, p, rows, col] = (pair - high.astype(F32)).astype(BF16)
                for kind in range(2):
                    for j in range(2):
                        mxf[kind, rows_at(t2 + j), col] = acc[kind][j]

    def rhs_pair(k, carry):
        waits = lax.rem(k * 2 * PLANES, LOAD) == 0

        @pl.when(waits)
        def _():
            for copy in s_loads(k * 2 * PLANES // LOAD):
                copy.wait()

        late = jnp.maximum(k - 1, 0)
        z_moments(halves[1], late, 2 * late + 1)
        rhs(halves[0], k, 2 * k)
        z_moments(halves[0], k, 2 * k)
        rhs(halves[1], k, 2 * k + 1)
        return carry

    lax.fori_loop(0, pairs, rhs_pair, 0)
    z_moments(halves[1], pairs - 1, chunks - 1)

    zcopies = [
        remote(mz.at[kind_to(gz, nz, o)], zbuf.at[o - 1], zs.at[o - 1], zr.at[o - 1],
               at("gz", lax.rem(gz + o, nz)))
        for o in range(1, nz)
    ]
    for copy in zcopies:
        copy.start()

    def solve_up(high, low):
        stack = jnp.concatenate([bz_ref[1], bz_ref[0], bz_ref[0]], 0)
        return jnp.dot(jnp.concatenate([high, low, high], 1), stack, preferred_element_type=F32)

    fold_h, fold_l = split(mxf[...].reshape(2 * north, upward))
    mx[...] = solve_up(fold_h, fold_l).reshape(2, north, upward) - 2.0 * mxu[...]

    pair = remote(mx.at[:, theirs, :], xpair, ps, pr, partner)
    pair.start()
    for kind in range(2):
        qown[kind] = dot(yw_ref[kind, 0], mx[0]) + dot(yw_ref[kind, 1], mx[1])
    qcopies = [
        remote(qown.at[kind_to(gy, ny, o)], qbuf.at[o - 1], qs.at[o - 1], qr.at[o - 1],
               at("gy", lax.rem(gy + o, ny)))
        for o in range(1, ny)
    ]
    for copy in qcopies:
        copy.start()
    xcopies = [
        remote(xtot.at[kind_to(chip, chips, o)], xbuf.at[o - 1], xs.at[o - 1], xr.at[o - 1],
               at("gx", lax.rem(chip + o, chips) * 2 + core))
        for o in range(1, chips)
    ]
    rcopies = [
        remote(rown.at[kind_to(gx, nx, o)], rbuf.at[o - 1], rs.at[o - 1], rr.at[o - 1],
               at("gx", lax.rem(gx + o, nx)))
        for o in range(1, nx)
    ]

    def send_chips():
        pair.wait()
        xtot[0] = mx[0, mine, :] + xpair[0]
        xtot[1] = mx[1, mine, :] + xpair[1]
        for copy in xcopies:
            copy.start()

    def send_edges():
        for copy in qcopies:
            copy.wait()
        qleft, qright = gather(gy, ny, qbuf)
        for kind in range(2):
            rown[kind] = stack_rows([qleft[kind:kind + 1], qright[kind:kind + 1]], upward)
        for copy in rcopies:
            copy.start()

    ecopies = [
        remote(eown.at[kind_to(gy, ny, o)], ebuf.at[o - 1], es.at[o - 1], er.at[o - 1],
               at("gy", lax.rem(gy + o, ny)))
        for o in range(1, ny)
    ]
    tcopies = [
        remote(town.at[kind_to(gx, nx, o)], tbuf.at[o - 1], ts.at[o - 1], tr.at[o - 1],
               at("gx", lax.rem(gx + o, nx)))
        for o in range(1, nx)
    ]

    def z_rows():
        for copy in zcopies:
            copy.wait()
        for m, value in enumerate(gather(gz, nz, zbuf)):
            zpad[m, 0:east] = value
        for kind in range(2):
            eown[kind] = dot(yw_ref[kind, 0], zpad[0], NT) + dot(yw_ref[kind, 1], zpad[1], NT)
        for copy in ecopies:
            copy.start()
        for m in range(2):
            face[m] = dot(zpad[m, 0:east], by_ref[...])

    def z_planes():
        for copy in ecopies:
            copy.wait()
        eleft, eright = gather(gy, ny, ebuf)
        value = [
            face[m] + (dot(eleft, yw_ref[1, m], TN) + dot(eright, yw_ref[0, m], TN))[0:east]
            for m in range(2)
        ]
        for kind in range(2):
            town[kind] = dot(xw_ref[kind, 0], value[0]) + dot(xw_ref[kind, 1], value[1])
        for copy in tcopies:
            copy.start()
        for m in range(2):
            face[m] = dot(bx_ref[...], value[m])

    part = east // 2
    ycopies = [
        [
            remote(my.at[kind_to(gy, ny, o), pl.ds(n * part, part)], ybuf.at[o - 1, pl.ds(n * part, part)],
                   ys.at[n, o - 1], yr.at[n, o - 1], at("gy", lax.rem(gy + o, ny)))
            for o in range(1, ny)
        ]
        for n in range(2)
    ]

    def send_rows(n):
        for copy in ycopies[n]:
            copy.start()

    def multiply(source, k, target):
        high_ref, low_ref = source
        target[...] = solve_up(
            high_ref[k].reshape(PLANES * north, upward), low_ref[k].reshape(PLANES * north, upward))

    def finish(source, c):
        base = pl.multiple_of(c * PLANES, PLANES)
        for l in range(tiles):
            col = cols(l)
            sums = [[None] * PLANES for _ in range(2)]
            for t in range(steps):
                w = [ytab_ref[kind, rows_at(t)] for kind in range(2)]
                for p in range(PLANES):
                    i = base + p
                    own = u_v[i + 1, t, :, col]
                    g = source[p * north + t * SUB:p * north + (t + 1) * SUB, col] - 2.0 * own
                    g_v[i, t, :, col] = g
                    for kind in range(2):
                        term = w[kind] * g
                        sums[kind][p] = term if t == 0 else sums[kind][p] + term
            for kind in range(2):
                for p in range(PLANES):
                    sg_ref[kind, base + p, :, col] = sums[kind][p]
                my[kind, pl.ds(base, PLANES), col] = stack_rows(
                    [jnp.sum(sums[kind][p], 0, keepdims=True) for p in range(PLANES)])

    def solve_pair(k, carry):
        @pl.when(k == min(1, pairs - 1))
        def _():
            send_chips()

        @pl.when(k == max(pairs - 2, 0))
        def _():
            z_rows()

        @pl.when(k == pairs - 1)
        def _():
            send_rows(0)
            send_edges()

        multiply(halves[0], k, y0)
        finish(y1, jnp.maximum(2 * k - 1, 0))
        multiply(halves[1], k, y1)
        finish(y0, 2 * k)
        return carry

    lax.fori_loop(0, pairs, solve_pair, 0)
    finish(y1, chunks - 1)

    send_rows(1)
    z_planes()

    for copy in xcopies:
        copy.wait()
    px, sx = gather(chip, chips, xbuf)
    first = jnp.where(core == 0, 1.0, 0.0).astype(F32)
    second = 1.0 - first
    xback[0] = px + first * mx[0, mine, :]
    xback[1] = sx + second * mx[1, mine, :]
    back = remote(xback, cx_ref.at[:, mine, :], bs, br, partner)
    back.start()
    cx_ref[0, mine, :] = px + second * xpair[0]
    cx_ref[1, mine, :] = sx + first * xpair[1]
    for copy in rcopies:
        copy.wait()
    rleft, rright = gather(gx, nx, rbuf)
    rright = rright + rown[1]
    back.wait()
    wy = wy_ref[...]
    by = by_ref[...]
    cx_ref[0] = dot(by, cx_ref[0]) + dot(wy, rleft, TN)
    cx_ref[1] = dot(by, cx_ref[1] + mx[1]) + dot(wy, rright, TN)

    for copy in tcopies:
        copy.wait()
    tleft, tright = gather(gx, nx, tbuf)
    for m in range(2):
        value = face[m] + dot(xw_ref[1, m], tleft, TN) + dot(xw_ref[0, m], tright, TN)
        high = value.astype(BF16).astype(F32)
        cz_ref[:, 3 * m, :] = high
        cz_ref[:, 3 * m + 1, :] = (value - high).astype(BF16).astype(F32)
        cz_ref[:, 3 * m + 2, :] = high
        cz_ref[:, 6 + m, :] = jnp.zeros_like(value)

    for n in range(2):
        for copy in ycopies[n]:
            copy.wait()
    left, right = gather(gy, ny, ybuf)
    cy_ref[0] = left
    cy_ref[1] = right


def local_pass(u, s, tables, sizes):
    east, north, upward = u.shape
    nx, ny, nz = sizes
    steps = north // SUB
    pairs = east // (2 * PLANES)
    blocks = east // LOAD
    chips = nx // 2
    half = north // 2
    vmem = pl.BlockSpec(memory_space=pltpu.VMEM)
    smem = pl.BlockSpec(memory_space=pltpu.SMEM)
    hbm = pl.BlockSpec(memory_space=pltpu.HBM)
    dma = pltpu.SemaphoreType.DMA

    def buf(*dims):
        return pltpu.VMEM(dims, F32)

    def halves():
        return pltpu.VMEM((pairs, PLANES, north, upward), BF16)

    names = ("bz", "zmom", "y", "yw", "xw", "wy", "by", "bx", "zadd")
    return pl.pallas_call(
        functools.partial(local_kernel, sizes, u.shape, tables["factors"]),
        name="local",
        out_shape=(
            buf(east, steps, SUB, upward),
            buf(east + 2, steps, SUB, upward),
            buf(2, east, SUB, upward),
            buf(east, SUB, north),
            buf(2, east, upward),
            buf(2, north, upward),
            buf(2, north, LANES),
            pltpu.VMEM((SUB, upward), BF16),
        ),
        in_specs=[hbm, hbm] + [hbm] * len(names) + [smem],
        out_specs=(vmem,) * 8,
        scratch_shapes=[
            pltpu.VMEM((2, upward, upward), BF16), pltpu.VMEM((upward, LANES), BF16),
            buf(2, 2, SUB, north), buf(2, 2, SUB, east), buf(SUB, north), buf(north, north), buf(east, east),
            dma((len(names),)),
            buf(east, steps, SUB, upward),
            halves(), halves(), halves(), halves(),
            buf(PLANES * north, upward), buf(PLANES * north, upward),
            buf(2, east, upward),
            buf(2, north, upward), buf(2, north, upward), buf(2, north, upward),
            buf(2, east, upward), buf(2, east, north),
            buf(nz - 1, east, north), buf(2, LANES, north), buf(ny - 1, east, upward),
            buf(2, half, upward), buf(2, half, upward), buf(chips - 1, half, upward), buf(2, half, upward),
            buf(2, SUB, LANES), buf(ny - 1, SUB, LANES),
            buf(2, SUB, upward), buf(ny - 1, SUB, upward),
            buf(2, SUB, upward), buf(nx - 1, SUB, upward),
            buf(2, SUB, north), buf(nx - 1, SUB, north), buf(2, east, north),
            dma((blocks, SUB)), dma((blocks, SUB)),
            dma((4,)), dma((4,)),
            dma((nz - 1,)), dma((nz - 1,)),
            dma((2, ny - 1)), dma((2, ny - 1)),
            dma, dma,
            dma((chips - 1,)), dma((chips - 1,)),
            dma, dma,
            dma((ny - 1,)), dma((ny - 1,)),
            dma((ny - 1,)), dma((ny - 1,)),
            dma((nx - 1,)), dma((nx - 1,)),
            dma((nx - 1,)), dma((nx - 1,)),
        ],
        compiler_params=pltpu.CompilerParams(
            collective_id=0, has_side_effects=True, vmem_limit_bytes=LOCAL_VMEM),
    )(*[pltpu.with_memory_space_constraint(a, pltpu.HBM) for a in [u, s] + [tables[name] for name in names + ("x",)]])


LOCAL_VMEM = 34 * 2**20
FINAL_VMEM = 24 * 2**20


def final_kernel(
    shape,
    g_v, u_v, sg_ref, cz_ref, cy_ref, cx_ref, zadd_ref, ytab_ref, xtab_ref,
    o_ref,
    edge_v, o_v, osem,
):
    gx, gy, gz = lax.axis_index("gx"), lax.axis_index("gy"), lax.axis_index("gz")
    east, north, upward = shape
    tiles = upward // LANES
    steps = north // SUB
    chunks = east // PLANES

    def stores(c):
        rows = pl.ds(c * PLANES, PLANES)
        return [
            pltpu.make_async_copy(
                o_v.at[rows, :, k, :], o_ref.at[rows, pl.ds(k * steps, steps), :], osem.at[c, k])
            for k in range(SUB)
        ]

    edge_v[...] = cx_ref[...]
    zadd = zadd_ref[...]
    sub = lax.broadcasted_iota(jnp.int32, (SUB, LANES), 0)

    def scan(value, backward):
        def shifted(x, d):
            if backward:
                return jnp.where(sub < SUB - d, pltpu.roll(x, SUB - d, 0), 0.0)
            return jnp.where(sub >= d, pltpu.roll(x, d, 0), 0.0)

        for d in (1, 2, 4):
            value = value + shifted(value, d)
        return shifted(value, 1)

    def step(c, carry):
        base = pl.multiple_of(c * PLANES, PLANES)
        wx = [[xtab_ref[kind, gx * east + base + p] for p in range(PLANES)] for kind in range(2)]
        add = []
        for p in range(PLANES):
            cz = cz_ref[base + p].T.astype(BF16)
            add.append(jnp.dot(cz, zadd, preferred_element_type=F32))
        for l in range(tiles):
            col = slice(l * LANES, (l + 1) * LANES)
            edge = [cy_ref[kind, pl.ds(base, PLANES), col] for kind in range(2)]
            low, high = [], []
            for p in range(PLANES):
                su, sv = sg_ref[0, base + p, :, col], sg_ref[1, base + p, :, col]
                low.append(scan(su, False) + edge[0][p:p + 1])
                high.append(scan(sv, True) + edge[1][p:p + 1] + sv)
            for t in range(steps):
                row = slice(t * SUB, (t + 1) * SUB)
                wu, wv = ytab_ref[0, row], ytab_ref[1, row]
                below, above = edge_v[0, row, col], edge_v[1, row, col]
                for p in range(PLANES):
                    i = base + p
                    g = g_v[i, t, :, col]
                    low[p] = low[p] + wu * g
                    high[p] = high[p] - wv * g
                    h = wv * low[p] + wu * high[p]
                    below = below + wx[0][p] * h
                    above = above - wx[1][p] * h
                    o_v[i, t, :, col] = (
                        u_v[i + 1, t, :, col] + add[p][row, col] + (wx[1][p] * below + wx[0][p] * above))
                edge_v[0, row, col] = below
                edge_v[1, row, col] = above
        for copy in stores(c):
            copy.start()
        return carry

    lax.fori_loop(0, chunks, step, 0)
    for c in range(chunks):
        for copy in stores(c):
            copy.wait()


def final_pass(g, u, sg, cz, cy, cx, ytab, zadd, tables, shape):
    east, north, upward = shape
    steps = north // SUB
    chunks = east // PLANES
    vmem = pl.BlockSpec(memory_space=pltpu.VMEM)
    smem = pl.BlockSpec(memory_space=pltpu.SMEM)
    return pl.pallas_call(
        functools.partial(final_kernel, shape),
        name="final",
        out_shape=jax.ShapeDtypeStruct(shape, F32),
        in_specs=[vmem] * 8 + [smem],
        out_specs=pl.BlockSpec(memory_space=pl.ANY),
        scratch_shapes=[
            pltpu.VMEM((2, north, upward), F32),
            pltpu.VMEM((east, steps, SUB, upward), F32),
            pltpu.SemaphoreType.DMA((chunks, SUB)),
        ],
        compiler_params=pltpu.CompilerParams(vmem_limit_bytes=FINAL_VMEM),
    )(g, u, sg, cz, cy, cx, zadd, ytab, tables["x"])


def local(sizes, u, s):
    tables = make_tables(u.shape, sizes)
    g, padded, *faces = local_pass(u, s, tables, sizes)
    return final_pass(g, padded, *faces, tables, u.shape)


def solution(mesh):
    sizes = tuple(mesh.shape[name] for name in ("gx", "gy", "gz"))
    spec = P("gx", "gy", "gz")
    return jax.shard_map(
        functools.partial(local, sizes), mesh=mesh, in_specs=(spec, spec), out_specs=spec, check_vma=False
    )
```

```python
import functools

import jax
import jax.numpy as jnp
import numpy as np
from jax import lax
from jax.experimental import pallas as pl
from jax.experimental.pallas import tpu as pltpu
from jax.sharding import PartitionSpec as P

MESH = pl.DeviceIdType.MESH
HIGH = lax.Precision.HIGHEST
F32 = jnp.float32
BF16 = jnp.bfloat16
LANES = 128
SUB = 8


def generators(whole, factor):
    half = 0.5 * factor
    theta = np.arccosh(1.0 + 0.5 / half)
    scale = np.sqrt(1.0 / (half * np.sinh(theta) * np.sinh((whole + 1) * theta)))
    index = np.arange(whole, dtype=np.float64)
    return np.sinh((index + 1) * theta) * scale, np.sinh((whole - index) * theta) * scale


def diagonal_blocks(u, v, members):
    extent = u.shape[0] // members
    blocks = []
    for member in range(members):
        part = slice(member * extent, (member + 1) * extent)
        own_u, own_v = u[part], v[part]
        lower = np.outer(own_v, own_u)
        blocks.append(np.where(np.tri(extent, dtype=bool), lower, lower.T))
    return np.stack(blocks)


def split_bf16(values):
    high = values.astype(np.float32).astype(BF16)
    low = (values - high.astype(np.float64)).astype(np.float32).astype(BF16)
    return np.asarray(high), np.asarray(low)


def split(values):
    high = values.astype(BF16)
    return high, (values - high.astype(F32)).astype(BF16)


def make_tables(shape, members):
    east, north, upward = shape
    wholes = [extent * count for extent, count in zip(shape, members)]
    factors = [float(whole * whole // 4) for whole in wholes]
    order = np.arange(north)
    order = (north // SUB) * (order % SUB) + order // SUB

    ux, vx = generators(wholes[0], factors[0])
    uy, vy = generators(wholes[1], factors[1])
    uz, vz = generators(wholes[2], factors[2])
    tables = {"factors": factors}
    tables["x"] = np.stack([ux, vx]).astype(np.float32)

    own = np.stack([w.reshape(members[1], north)[:, order] for w in (uy, vy)], 1)
    tables["y"] = np.repeat(own[..., None], LANES, -1).astype(np.float32)
    by = diagonal_blocks(uy, vy, members[1])[:, order][:, :, order]
    tables["by"] = by.astype(np.float32)
    tables["bx"] = diagonal_blocks(ux, vx, members[0]).astype(np.float32)
    yw = np.zeros((members[1], 2, 2, SUB, north), np.float32)
    xw = np.zeros((members[0], 2, 2, SUB, east), np.float32)
    for slot in range(2):
        yw[:, :, slot, slot] = own
        for kind, w in enumerate((ux, vx)):
            xw[:, kind, slot, slot] = w.reshape(members[0], east)
    tables["yw"], tables["xw"] = yw, xw
    yuh, yul = [a.astype(np.float32) for a in split_bf16(own[:, 0].astype(np.float64))]
    yvh, yvl = [a.astype(np.float32) for a in split_bf16(own[:, 1].astype(np.float64))]
    zero = np.zeros_like(yuh)
    tables["yadd"] = np.stack([yvh, yvl, yvh, yuh, yul, yuh, zero, zero], 1)

    bzh, bzl = split_bf16(diagonal_blocks(uz, vz, members[2]))
    tables["bz"] = np.stack([bzh, bzl], 1)
    zu, zv = uz.reshape(members[2], upward), vz.reshape(members[2], upward)
    uh, ul = split_bf16(zu)
    vh, vl = split_bf16(zv)
    zero = np.zeros_like(uh)
    tables["zmom"] = np.stack([uh, ul, vh, vl] + [zero] * (LANES - 4), 2)
    tables["zadd"] = np.stack([vh, vh, vl, uh, uh, ul, zero, zero], 1)
    return tables


def at(axis, index):
    return {axis: index}


def greet(partners):
    barrier = pltpu.get_barrier_semaphore()
    for partner in partners:
        pl.semaphore_signal(barrier, inc=1, device_id=partner, device_id_type=MESH)
    pl.semaphore_wait(barrier, len(partners))


def remote(src, dst, send, recv, partner):
    return pltpu.make_async_remote_copy(
        src_ref=src, dst_ref=dst, send_sem=send, recv_sem=recv, device_id=partner, device_id_type=MESH
    )


def kind_to(me, count, o):
    return jnp.where(lax.rem(me + o, count) > me, 0, 1)


def gather(me, count, buf):
    left = right = None
    for o in range(1, count):
        low = jnp.where(lax.rem(me + count - o, count) < me, 1.0, 0.0).astype(F32)
        piece = buf[o - 1]
        left = piece * low if left is None else left + piece * low
        right = piece * (1.0 - low) if right is None else right + piece * (1.0 - low)
    return left, right


NN = (((1,), (0,)), ((), ()))
NT = (((1,), (1,)), ((), ()))
TN = (((0,), (0,)), ((), ()))


def dot(a, b, dims=NN):
    if dims == TN:
        return lax.dot_general(a, b, dims, precision=HIGH, preferred_element_type=F32)
    ah, al = split(a)
    bh, bl = split(b)
    left = jnp.concatenate([ah, al, ah], 1)
    right = jnp.concatenate([bl, bh, bh], dims[0][1][0])
    return lax.dot_general(left, right, dims, preferred_element_type=F32)


PLANES = 8
LOAD = 16


def stack_rows(rows, width=LANES):
    sub = lax.broadcasted_iota(jnp.int32, (SUB, width), 0)
    out = jnp.zeros((SUB, width), F32)
    for p, row in enumerate(rows):
        out = jnp.where(sub == p, row, out)
    return out


def local_kernel(
    sizes, shape, factors,
    u_ref, s_ref, bz_hbm, zmom_hbm, ytab_hbm, yw_hbm, xw_hbm, by_hbm, bx_hbm, zadd_hbm, xtab_ref,
    g_v, cz_ref, cy_ref, cx_ref, zadd_ref,
    bz_ref, zmom_ref, yw_ref, xw_ref, by_ref, bx_ref, tsem,
    u_v, sg_ref, ytab_ref, edge_v, xland, s_v, fh0, fl0, fh1, fl1, y0, y1, hy, mxf, mxu, mx, my, mz,
    zbuf, zpad, ybuf, xpair, xtot, xbuf, xback, eown, ebuf, qown, qbuf, rown, rbuf, town, tbuf, face,
    usem, ssem, hs, hr, zs, zr, ys, yr, ps, pr, xs, xr, bs, br, es, er, qs, qr, rs, rr, ts, tr,
):
    gx, gy, gz = lax.axis_index("gx"), lax.axis_index("gy"), lax.axis_index("gz")
    nx, ny, nz = sizes
    east, north, upward = shape
    tiles = upward // LANES
    steps = north // SUB
    chunks = east // PLANES
    pairs = chunks // 2
    blocks = east // LOAD
    rx, ry, _ = factors
    chips = nx // 2
    half = north // 2
    chip, core = gx // 2, lax.rem(gx, 2)
    mine = pl.ds(pl.multiple_of(core * half, half), half)
    theirs = pl.ds(pl.multiple_of((1 - core) * half, half), half)
    partner = at("gx", chip * 2 + 1 - core)

    def u_loads(b):
        rows = pl.ds(b * LOAD, LOAD)
        return [
            pltpu.make_async_copy(
                u_ref.at[rows, pl.ds(k * steps, steps), :], u_v.at[pl.ds(1 + b * LOAD, LOAD), :, k, :],
                usem.at[b, k])
            for k in range(SUB)
        ]

    def s_loads(b):
        rows = pl.ds(b * LOAD, LOAD)
        return [
            pltpu.make_async_copy(
                s_ref.at[rows, pl.ds(k * steps, steps), :], s_v.at[rows, :, k, :], ssem.at[b, k])
            for k in range(SUB)
        ]

    early = sorted({0, blocks - 1})
    for b in early + [b for b in range(blocks) if b not in early]:
        for copy in u_loads(b):
            copy.start()
    table_loads = [
        pltpu.make_async_copy(hbm.at[index], ref, tsem.at[n])
        for n, (hbm, index, ref) in enumerate((
            (bz_hbm, gz, bz_ref), (zmom_hbm, gz, zmom_ref), (ytab_hbm, gy, ytab_ref), (yw_hbm, gy, yw_ref),
            (xw_hbm, gx, xw_ref), (by_hbm, gy, by_ref), (bx_hbm, gx, bx_ref),
            (zadd_hbm, gz, zadd_ref)))
    ]
    for copy in table_loads:
        copy.start()

    def ring(axis, me, count):
        return [at(axis, lax.rem(me + o, count)) for o in range(1, count)]

    greet(ring("gx", gx, nx) + ring("gy", gy, ny) + ring("gz", gz, nz))

    xr_, xl_ = lax.rem(gx + 1, nx), lax.rem(gx + nx - 1, nx)
    yr_, yl_ = lax.rem(gy + 1, ny), lax.rem(gy + ny - 1, ny)
    halos = [
        remote(u_ref.at[:, north - 1, :], hy.at[0], hs.at[2], hr.at[2], at("gy", yr_)),
        remote(u_ref.at[:, 0, :], hy.at[1], hs.at[3], hr.at[3], at("gy", yl_)),
        remote(u_v.at[east], u_v.at[0], hs.at[0], hr.at[0], at("gx", xr_)),
        remote(u_v.at[1], u_v.at[east + 1], hs.at[1], hr.at[1], at("gx", xl_)),
    ]
    for copy in halos[:2]:
        copy.start()
    for b in early:
        for copy in u_loads(b):
            copy.wait()
    for copy in halos[2:]:
        copy.start()
    for b in range(blocks):
        for copy in s_loads(b):
            copy.start()

    sub = lax.broadcasted_iota(jnp.int32, (SUB, LANES), 0)

    def cols(l):
        return slice(l * LANES, (l + 1) * LANES)

    def rows_at(t):
        return slice(t * SUB, (t + 1) * SUB)

    mxu[...] = jnp.zeros_like(mxu)
    mxf[...] = jnp.zeros_like(mxf)
    zpad[...] = jnp.zeros_like(zpad)

    def weights(base):
        return [[xtab_ref[kind, gx * east + base + p] for p in range(PLANES)] for kind in range(2)]

    def pre(c, carry):
        block = c * PLANES // LOAD
        waits = lax.rem(c * PLANES, LOAD) == 0
        for b in early:
            waits = jnp.logical_and(waits, block != b)

        @pl.when(waits)
        def _():
            for copy in u_loads(block):
                copy.wait()

        base = c * PLANES
        w = weights(base)
        for l in range(tiles):
            for t in range(steps):
                acc = [mxu[kind, rows_at(t), cols(l)] for kind in range(2)]
                for p in range(PLANES):
                    own = u_v[base + p + 1, t, :, cols(l)]
                    for kind in range(2):
                        acc[kind] = acc[kind] + w[kind][p] * own
                for kind in range(2):
                    mxu[kind, rows_at(t), cols(l)] = acc[kind]
        return carry

    lax.fori_loop(0, chunks, pre, 0)

    for copy in halos:
        copy.wait()
    before = jnp.where(gx > 0, 1.0, 0.0).astype(F32)
    after = jnp.where(gx < nx - 1, 1.0, 0.0).astype(F32)
    south = jnp.where(gy > 0, 1.0, 0.0).astype(F32)
    nord = jnp.where(gy < ny - 1, 1.0, 0.0).astype(F32)
    u_v[0] = u_v[0] * before
    u_v[east + 1] = u_v[east + 1] * after

    for copy in table_loads:
        copy.wait()
    zmom = zmom_ref[...]
    halves = ((fh0, fl0), (fh1, fl1))

    def z_moments(source, k, c):
        flat = jnp.concatenate([f[k].reshape(PLANES * north, upward) for f in source], 1)
        mom = jnp.dot(flat, jnp.concatenate([zmom, zmom], 0), preferred_element_type=F32)
        across = [mom[p * north:(p + 1) * north].T for p in range(PLANES)]
        for kind in range(2):
            mz[kind, pl.ds(pl.multiple_of(c * PLANES, PLANES), PLANES), :] = stack_rows(
                [a[2 * kind:2 * kind + 1] + a[2 * kind + 1:2 * kind + 2] for a in across])

    def rhs(target, k, c):
        high_ref, low_ref = target
        base = pl.multiple_of(c * PLANES, PLANES)
        w = weights(base)
        for l in range(tiles):
            col = cols(l)
            edge = [hy[0, pl.ds(base, PLANES), col] * south, hy[1, pl.ds(base, PLANES), col] * nord]
            for t2 in range(0, steps, 2):
                acc = [[mxf[kind, rows_at(t2 + j), col] for j in range(2)] for kind in range(2)]
                column = [[u_v[base + p, t2 + j, :, col] for p in range(PLANES + 2)] for j in range(2)]
                for p in range(PLANES):
                    i = base + p
                    if t2 == 0:
                        below = pltpu.roll(u_v[i + 1, steps - 1, :, col], 1, 0)
                        below = jnp.where(sub == 0, edge[0][p:p + 1], below)
                    else:
                        below = u_v[i + 1, t2 - 1, :, col]
                    if t2 == steps - 2:
                        above = pltpu.roll(u_v[i + 1, 0, :, col], SUB - 1, 0)
                        above = jnp.where(sub == SUB - 1, edge[1][p:p + 1], above)
                    else:
                        above = u_v[i + 1, t2 + 2, :, col]
                    out = []
                    for j in range(2):
                        own = column[j][p + 1]
                        across = column[j][p] + column[j][p + 2]
                        along = (below + column[1][p + 1]) if j == 0 else (column[0][p + 1] + above)
                        if rx == ry:
                            spread = rx * ((across + along) + (2.0 / rx - 4.0) * own)
                        else:
                            spread = rx * across + ry * along + (2.0 - 2.0 * rx - 2.0 * ry) * own
                        f = s_v[i, t2 + j, :, col] + spread
                        for kind in range(2):
                            acc[kind][j] = acc[kind][j] + w[kind][p] * f
                        out.append(f)
                    pair = jnp.concatenate(out, 0)
                    high = pair.astype(BF16)
                    rows = slice(t2 * SUB, (t2 + 2) * SUB)
                    high_ref[k, p, rows, col] = high
                    low_ref[k, p, rows, col] = (pair - high.astype(F32)).astype(BF16)
                for kind in range(2):
                    for j in range(2):
                        mxf[kind, rows_at(t2 + j), col] = acc[kind][j]

    def rhs_pair(k, carry):
        waits = lax.rem(k * 2 * PLANES, LOAD) == 0

        @pl.when(waits)
        def _():
            for copy in s_loads(k * 2 * PLANES // LOAD):
                copy.wait()

        late = jnp.maximum(k - 1, 0)
        z_moments(halves[1], late, 2 * late + 1)
        rhs(halves[0], k, 2 * k)
        z_moments(halves[0], k, 2 * k)
        rhs(halves[1], k, 2 * k + 1)
        return carry

    lax.fori_loop(0, pairs, rhs_pair, 0)
    z_moments(halves[1], pairs - 1, chunks - 1)

    zcopies = [
        remote(mz.at[kind_to(gz, nz, o)], zbuf.at[o - 1], zs.at[o - 1], zr.at[o - 1],
               at("gz", lax.rem(gz + o, nz)))
        for o in range(1, nz)
    ]
    for copy in zcopies:
        copy.start()

    def solve_up(high, low):
        stack = jnp.concatenate([bz_ref[1], bz_ref[0], bz_ref[0]], 0)
        return jnp.dot(jnp.concatenate([high, low, high], 1), stack, preferred_element_type=F32)

    fold_h, fold_l = split(mxf[...].reshape(2 * north, upward))
    mx[...] = solve_up(fold_h, fold_l).reshape(2, north, upward) - 2.0 * mxu[...]

    pair = remote(mx.at[:, theirs, :], xpair, ps, pr, partner)
    pair.start()
    for kind in range(2):
        qown[kind] = dot(yw_ref[kind, 0], mx[0]) + dot(yw_ref[kind, 1], mx[1])
    qcopies = [
        remote(qown.at[kind_to(gy, ny, o)], qbuf.at[o - 1], qs.at[o - 1], qr.at[o - 1],
               at("gy", lax.rem(gy + o, ny)))
        for o in range(1, ny)
    ]
    for copy in qcopies:
        copy.start()
    xcopies = [
        remote(xtot.at[kind_to(chip, chips, o)], xbuf.at[o - 1], xs.at[o - 1], xr.at[o - 1],
               at("gx", lax.rem(chip + o, chips) * 2 + core))
        for o in range(1, chips)
    ]
    rcopies = [
        remote(rown.at[kind_to(gx, nx, o)], rbuf.at[o - 1], rs.at[o - 1], rr.at[o - 1],
               at("gx", lax.rem(gx + o, nx)))
        for o in range(1, nx)
    ]

    def send_chips():
        pair.wait()
        xtot[0] = mx[0, mine, :] + xpair[0]
        xtot[1] = mx[1, mine, :] + xpair[1]
        for copy in xcopies:
            copy.start()

    def send_edges():
        for copy in qcopies:
            copy.wait()
        qleft, qright = gather(gy, ny, qbuf)
        for kind in range(2):
            rown[kind] = stack_rows([qleft[kind:kind + 1], qright[kind:kind + 1]], upward)
        for copy in rcopies:
            copy.start()

    ecopies = [
        remote(eown.at[kind_to(gy, ny, o)], ebuf.at[o - 1], es.at[o - 1], er.at[o - 1],
               at("gy", lax.rem(gy + o, ny)))
        for o in range(1, ny)
    ]
    tcopies = [
        remote(town.at[kind_to(gx, nx, o)], tbuf.at[o - 1], ts.at[o - 1], tr.at[o - 1],
               at("gx", lax.rem(gx + o, nx)))
        for o in range(1, nx)
    ]

    def z_rows():
        for copy in zcopies:
            copy.wait()
        for m, value in enumerate(gather(gz, nz, zbuf)):
            zpad[m, 0:east] = value
        for kind in range(2):
            eown[kind] = dot(yw_ref[kind, 0], zpad[0], NT) + dot(yw_ref[kind, 1], zpad[1], NT)
        for copy in ecopies:
            copy.start()
        for m in range(2):
            face[m] = dot(zpad[m, 0:east], by_ref[...])

    def z_planes():
        for copy in ecopies:
            copy.wait()
        eleft, eright = gather(gy, ny, ebuf)
        value = [
            face[m] + (dot(eleft, yw_ref[1, m], TN) + dot(eright, yw_ref[0, m], TN))[0:east]
            for m in range(2)
        ]
        for kind in range(2):
            town[kind] = dot(xw_ref[kind, 0], value[0]) + dot(xw_ref[kind, 1], value[1])
        for copy in tcopies:
            copy.start()
        for m in range(2):
            face[m] = dot(bx_ref[...], value[m])

    parts = (max(chunks - 3, 1) * PLANES, east)
    ycopies = [
        [
            remote(my.at[kind_to(gy, ny, o), pl.ds(n * parts[0], parts[n] - n * parts[0])],
                   ybuf.at[o - 1, pl.ds(n * parts[0], parts[n] - n * parts[0])],
                   ys.at[n, o - 1], yr.at[n, o - 1], at("gy", lax.rem(gy + o, ny)))
            for o in range(1, ny)
        ]
        for n in range(2)
    ]

    def send_rows(n):
        for copy in ycopies[n]:
            copy.start()

    def multiply(source, k, target):
        high_ref, low_ref = source
        target[...] = solve_up(
            high_ref[k].reshape(PLANES * north, upward), low_ref[k].reshape(PLANES * north, upward))

    def finish(source, c):
        base = pl.multiple_of(c * PLANES, PLANES)
        for l in range(tiles):
            col = cols(l)
            sums = [[None] * PLANES for _ in range(2)]
            for t in range(steps):
                w = [ytab_ref[kind, rows_at(t)] for kind in range(2)]
                for p in range(PLANES):
                    i = base + p
                    own = u_v[i + 1, t, :, col]
                    g = source[p * north + t * SUB:p * north + (t + 1) * SUB, col] - 2.0 * own
                    g_v[i, t, :, col] = g
                    for kind in range(2):
                        term = w[kind] * g
                        sums[kind][p] = term if t == 0 else sums[kind][p] + term
            for kind in range(2):
                for p in range(PLANES):
                    sg_ref[kind, base + p, :, col] = sums[kind][p]
                my[kind, pl.ds(base, PLANES), col] = stack_rows(
                    [jnp.sum(sums[kind][p], 0, keepdims=True) for p in range(PLANES)])

    def solve_pair(k, carry):
        @pl.when(k == min(1, pairs - 1))
        def _():
            send_chips()

        @pl.when(k == max(pairs - 2, 0))
        def _():
            z_rows()

        @pl.when(k == pairs - 1)
        def _():
            send_rows(0)
            send_edges()

        multiply(halves[0], k, y0)
        finish(y1, jnp.maximum(2 * k - 1, 0))
        multiply(halves[1], k, y1)
        finish(y0, 2 * k)
        return carry

    lax.fori_loop(0, pairs, solve_pair, 0)
    finish(y1, chunks - 1)

    send_rows(1)
    z_planes()

    by = by_ref[...]
    edge_v[0] = jnp.zeros((north, upward), F32)
    edge_v[1] = dot(by, mx[1])

    def scan(value, backward):
        def shifted(x, d):
            if backward:
                return jnp.where(sub < SUB - d, pltpu.roll(x, SUB - d, 0), 0.0)
            return jnp.where(sub >= d, pltpu.roll(x, d, 0), 0.0)

        for d in (1, 2, 4):
            value = value + shifted(value, d)
        return shifted(value, 1)

    first = jnp.where(core == 0, 1.0, 0.0).astype(F32)
    second = 1.0 - first
    back = remote(xback, xland, bs, br, partner)

    def return_chips():
        for copy in xcopies:
            copy.wait()
        px, sx = gather(chip, chips, xbuf)
        xback[0] = px + first * mx[0, mine, :]
        xback[1] = sx + second * mx[1, mine, :]
        back.start()
        cx_ref[0, mine, :] = px + second * xpair[0]
        cx_ref[1, mine, :] = sx + first * xpair[1]

    def sweep(c, carry):
        @pl.when(c == min(2, chunks - 1))
        def _():
            return_chips()

        base = pl.multiple_of(c * PLANES, PLANES)
        wx = weights(base)
        for l in range(tiles):
            col = cols(l)
            low, high = [], []
            for p in range(PLANES):
                su, sv = sg_ref[0, base + p, :, col], sg_ref[1, base + p, :, col]
                low.append(scan(su, False))
                high.append(scan(sv, True) + sv)
            for t in range(steps):
                wu, wv = ytab_ref[0, rows_at(t)], ytab_ref[1, rows_at(t)]
                below, above = edge_v[0, rows_at(t), col], edge_v[1, rows_at(t), col]
                for p in range(PLANES):
                    i = base + p
                    g = g_v[i, t, :, col]
                    low[p] = low[p] + wu * g
                    high[p] = high[p] - wv * g
                    h = wv * low[p] + wu * high[p]
                    below = below + wx[0][p] * h
                    above = above - wx[1][p] * h
                    g_v[i, t, :, col] = u_v[i + 1, t, :, col] + (wx[1][p] * below + wx[0][p] * above)
                edge_v[0, rows_at(t), col] = below
                edge_v[1, rows_at(t), col] = above
        return carry

    lax.fori_loop(0, chunks, sweep, 0)

    back.wait()
    cx_ref[0, theirs, :] = xland[0]
    cx_ref[1, theirs, :] = xland[1]
    cx_ref[0] = dot(by, cx_ref[0])
    cx_ref[1] = dot(by, cx_ref[1])

    for copy in tcopies:
        copy.wait()
    tleft, tright = gather(gx, nx, tbuf)
    for m in range(2):
        value = face[m] + dot(xw_ref[1, m], tleft, TN) + dot(xw_ref[0, m], tright, TN)
        high = value.astype(BF16).astype(F32)
        cz_ref[:, 3 * m, :] = high
        cz_ref[:, 3 * m + 1, :] = (value - high).astype(BF16).astype(F32)
        cz_ref[:, 3 * m + 2, :] = high
        cz_ref[:, 6 + m, :] = jnp.zeros_like(value)

    for copy in rcopies:
        copy.wait()
    rleft, rright = gather(gx, nx, rbuf)
    fixed = [dot(xw_ref[1, m], rleft, TN) + dot(xw_ref[0, m], rright, TN) for m in range(2)]
    for n in range(2):
        for copy in ycopies[n]:
            copy.wait()
    for m, face_y in enumerate(gather(gy, ny, ybuf)):
        value = dot(bx_ref[...], face_y) + fixed[m]
        high = value.astype(BF16).astype(F32)
        cy_ref[:, 3 * m, :] = high
        cy_ref[:, 3 * m + 1, :] = high
        cy_ref[:, 3 * m + 2, :] = (value - high).astype(BF16).astype(F32)
        cy_ref[:, 6 + m, :] = jnp.zeros_like(value)


def local_pass(u, s, tables, sizes):
    east, north, upward = u.shape
    nx, ny, nz = sizes
    steps = north // SUB
    pairs = east // (2 * PLANES)
    blocks = east // LOAD
    chips = nx // 2
    half = north // 2
    vmem = pl.BlockSpec(memory_space=pltpu.VMEM)
    smem = pl.BlockSpec(memory_space=pltpu.SMEM)
    hbm = pl.BlockSpec(memory_space=pltpu.HBM)
    dma = pltpu.SemaphoreType.DMA

    def buf(*dims):
        return pltpu.VMEM(dims, F32)

    def halves():
        return pltpu.VMEM((pairs, PLANES, north, upward), BF16)

    names = ("bz", "zmom", "y", "yw", "xw", "by", "bx", "zadd")
    return pl.pallas_call(
        functools.partial(local_kernel, sizes, u.shape, tables["factors"]),
        name="local",
        out_shape=(
            buf(east, steps, SUB, upward),
            buf(east, SUB, north),
            buf(east, SUB, upward),
            buf(2, north, upward),
            pltpu.VMEM((SUB, upward), BF16),
        ),
        in_specs=[hbm, hbm] + [hbm] * len(names) + [smem],
        out_specs=(vmem,) * 5,
        scratch_shapes=[
            pltpu.VMEM((2, upward, upward), BF16), pltpu.VMEM((upward, LANES), BF16),
            buf(2, 2, SUB, north), buf(2, 2, SUB, east), buf(north, north), buf(east, east),
            dma((len(names),)),
            buf(east + 2, steps, SUB, upward),
            buf(2, east, SUB, upward),
            buf(2, north, LANES),
            buf(2, north, upward),
            buf(2, half, upward),
            buf(east, steps, SUB, upward),
            halves(), halves(), halves(), halves(),
            buf(PLANES * north, upward), buf(PLANES * north, upward),
            buf(2, east, upward),
            buf(2, north, upward), buf(2, north, upward), buf(2, north, upward),
            buf(2, east, upward), buf(2, east, north),
            buf(nz - 1, east, north), buf(2, LANES, north), buf(ny - 1, east, upward),
            buf(2, half, upward), buf(2, half, upward), buf(chips - 1, half, upward), buf(2, half, upward),
            buf(2, SUB, LANES), buf(ny - 1, SUB, LANES),
            buf(2, SUB, upward), buf(ny - 1, SUB, upward),
            buf(2, SUB, upward), buf(nx - 1, SUB, upward),
            buf(2, SUB, north), buf(nx - 1, SUB, north), buf(2, east, north),
            dma((blocks, SUB)), dma((blocks, SUB)),
            dma((4,)), dma((4,)),
            dma((nz - 1,)), dma((nz - 1,)),
            dma((2, ny - 1)), dma((2, ny - 1)),
            dma, dma,
            dma((chips - 1,)), dma((chips - 1,)),
            dma, dma,
            dma((ny - 1,)), dma((ny - 1,)),
            dma((ny - 1,)), dma((ny - 1,)),
            dma((nx - 1,)), dma((nx - 1,)),
            dma((nx - 1,)), dma((nx - 1,)),
        ],
        compiler_params=pltpu.CompilerParams(
            collective_id=0, has_side_effects=True, vmem_limit_bytes=LOCAL_VMEM),
    )(*[pltpu.with_memory_space_constraint(a, pltpu.HBM) for a in [u, s] + [tables[name] for name in names + ("x",)]])


LOCAL_VMEM = 44 * 2**20
FINAL_VMEM = 24 * 2**20


def final_kernel(
    shape,
    t_v, cz_ref, cy_ref, cx_ref, zadd_ref, yadd_ref, xtab_ref,
    o_ref,
    o_v, osem,
):
    gx, gy = lax.axis_index("gx"), lax.axis_index("gy")
    east, north, upward = shape
    tiles = upward // LANES
    steps = north // SUB
    chunks = east // PLANES

    def stores(c):
        rows = pl.ds(c * PLANES, PLANES)
        return [
            pltpu.make_async_copy(
                o_v.at[rows, :, k, :], o_ref.at[rows, pl.ds(k * steps, steps), :], osem.at[c, k])
            for k in range(SUB)
        ]

    zadd = zadd_ref[...].astype(F32)
    yadd = yadd_ref[gy]

    def step(c, carry):
        base = pl.multiple_of(c * PLANES, PLANES)
        wx = [[xtab_ref[kind, gx * east + base + p] for p in range(PLANES)] for kind in range(2)]
        add = []
        for p in range(PLANES):
            left = jnp.concatenate([cz_ref[base + p], yadd], 0).T.astype(BF16)
            right = jnp.concatenate([zadd, cy_ref[base + p]], 0).astype(BF16)
            add.append(jnp.dot(left, right, preferred_element_type=F32))
        for l in range(tiles):
            col = slice(l * LANES, (l + 1) * LANES)
            for t in range(steps):
                row = slice(t * SUB, (t + 1) * SUB)
                below, above = cx_ref[0, row, col], cx_ref[1, row, col]
                for p in range(PLANES):
                    o_v[base + p, t, :, col] = (t_v[base + p, t, :, col] + add[p][row, col]) + (
                        wx[1][p] * below + wx[0][p] * above)
        for copy in stores(c):
            copy.start()
        return carry

    lax.fori_loop(0, chunks, step, 0)
    for c in range(chunks):
        for copy in stores(c):
            copy.wait()


def final_pass(t, cz, cy, cx, zadd, tables, shape):
    east, north, upward = shape
    steps = north // SUB
    chunks = east // PLANES
    vmem = pl.BlockSpec(memory_space=pltpu.VMEM)
    smem = pl.BlockSpec(memory_space=pltpu.SMEM)
    return pl.pallas_call(
        functools.partial(final_kernel, shape),
        name="final",
        out_shape=jax.ShapeDtypeStruct(shape, F32),
        in_specs=[vmem] * 6 + [smem],
        out_specs=pl.BlockSpec(memory_space=pl.ANY),
        scratch_shapes=[
            pltpu.VMEM((east, steps, SUB, upward), F32),
            pltpu.SemaphoreType.DMA((chunks, SUB)),
        ],
        compiler_params=pltpu.CompilerParams(vmem_limit_bytes=FINAL_VMEM),
    )(t, cz, cy, cx, zadd, tables["yadd"], tables["x"])


def local(sizes, u, s):
    tables = make_tables(u.shape, sizes)
    return final_pass(*local_pass(u, s, tables, sizes), tables, u.shape)


def solution(mesh):
    sizes = tuple(mesh.shape[name] for name in ("gx", "gy", "gz"))
    spec = P("gx", "gy", "gz")
    return jax.shard_map(
        functools.partial(local, sizes), mesh=mesh, in_specs=(spec, spec), out_specs=spec, check_vma=False
    )
```

```python
import functools

import jax
import jax.numpy as jnp
import numpy as np
from jax import lax
from jax.experimental import pallas as pl
from jax.experimental.pallas import tpu as pltpu
from jax.sharding import PartitionSpec as P

MESH = pl.DeviceIdType.MESH
HIGH = lax.Precision.HIGHEST
F32 = jnp.float32
BF16 = jnp.bfloat16
LANES = 128
SUB = 8


def generators(whole, factor):
    half = 0.5 * factor
    theta = np.arccosh(1.0 + 0.5 / half)
    scale = np.sqrt(1.0 / (half * np.sinh(theta) * np.sinh((whole + 1) * theta)))
    index = np.arange(whole, dtype=np.float64)
    return np.sinh((index + 1) * theta) * scale, np.sinh((whole - index) * theta) * scale


def diagonal_blocks(u, v, members):
    extent = u.shape[0] // members
    blocks = []
    for member in range(members):
        part = slice(member * extent, (member + 1) * extent)
        own_u, own_v = u[part], v[part]
        lower = np.outer(own_v, own_u)
        blocks.append(np.where(np.tri(extent, dtype=bool), lower, lower.T))
    return np.stack(blocks)


def split_bf16(values):
    high = values.astype(np.float32).astype(BF16)
    low = (values - high.astype(np.float64)).astype(np.float32).astype(BF16)
    return np.asarray(high), np.asarray(low)


def split(values):
    high = values.astype(BF16)
    return high, (values - high.astype(F32)).astype(BF16)


def make_tables(shape, members):
    east, north, upward = shape
    wholes = [extent * count for extent, count in zip(shape, members)]
    factors = [float(whole * whole // 4) for whole in wholes]
    order = np.arange(north)
    order = (north // SUB) * (order % SUB) + order // SUB

    ux, vx = generators(wholes[0], factors[0])
    uy, vy = generators(wholes[1], factors[1])
    uz, vz = generators(wholes[2], factors[2])
    tables = {"factors": factors}
    tables["x"] = np.stack([ux, vx]).astype(np.float32)

    own = np.stack([w.reshape(members[1], north)[:, order] for w in (uy, vy)], 1)
    tables["y"] = np.repeat(own[..., None], LANES, -1).astype(np.float32)
    by = diagonal_blocks(uy, vy, members[1])[:, order][:, :, order]
    tables["by"] = by.astype(np.float32)
    tables["bx"] = diagonal_blocks(ux, vx, members[0]).astype(np.float32)
    yw = np.zeros((members[1], 2, 2, SUB, north), np.float32)
    xw = np.zeros((members[0], 2, 2, SUB, east), np.float32)
    for slot in range(2):
        yw[:, :, slot, slot] = own
        for kind, w in enumerate((ux, vx)):
            xw[:, kind, slot, slot] = w.reshape(members[0], east)
    tables["yw"], tables["xw"] = yw, xw
    yuh, yul = [a.astype(np.float32) for a in split_bf16(own[:, 0].astype(np.float64))]
    yvh, yvl = [a.astype(np.float32) for a in split_bf16(own[:, 1].astype(np.float64))]
    zero = np.zeros_like(yuh)
    tables["yadd"] = np.stack([yvh, yvl, yvh, yuh, yul, yuh, zero, zero], 1)

    bzh, bzl = split_bf16(diagonal_blocks(uz, vz, members[2]))
    tables["bz"] = np.stack([bzh, bzl], 1)
    zu, zv = uz.reshape(members[2], upward), vz.reshape(members[2], upward)
    uh, ul = split_bf16(zu)
    vh, vl = split_bf16(zv)
    zero = np.zeros_like(uh)
    tables["zmom"] = np.stack([uh, ul, vh, vl] + [zero] * (LANES - 4), 2)
    tables["zadd"] = np.stack([vh, vh, vl, uh, uh, ul, zero, zero], 1)
    return tables


def at(axis, index):
    return {axis: index}


def greet(partners):
    barrier = pltpu.get_barrier_semaphore()
    for partner in partners:
        pl.semaphore_signal(barrier, inc=1, device_id=partner, device_id_type=MESH)
    pl.semaphore_wait(barrier, len(partners))


def remote(src, dst, send, recv, partner):
    return pltpu.make_async_remote_copy(
        src_ref=src, dst_ref=dst, send_sem=send, recv_sem=recv, device_id=partner, device_id_type=MESH
    )


def kind_to(me, count, o):
    return jnp.where(lax.rem(me + o, count) > me, 0, 1)


def gather(me, count, buf):
    left = right = None
    for o in range(1, count):
        low = jnp.where(lax.rem(me + count - o, count) < me, 1.0, 0.0).astype(F32)
        piece = buf[o - 1]
        left = piece * low if left is None else left + piece * low
        right = piece * (1.0 - low) if right is None else right + piece * (1.0 - low)
    return left, right


NN = (((1,), (0,)), ((), ()))
NT = (((1,), (1,)), ((), ()))
TN = (((0,), (0,)), ((), ()))


def dot(a, b, dims=NN):
    ah, al = split(a)
    bh, bl = split(b)
    if dims == TN:
        parts = [[x.astype(F32) for x in group] for group in ((ah, al, ah), (bl, bh, bh))]
        left, right = (jnp.concatenate(group + [jnp.zeros_like(group[0])], 0).astype(BF16) for group in parts)
        return lax.dot_general(left, right, dims, preferred_element_type=F32)
    left = jnp.concatenate([ah, al, ah], 1)
    right = jnp.concatenate([bl, bh, bh], dims[0][1][0])
    return lax.dot_general(left, right, dims, preferred_element_type=F32)


PLANES = 8
LOAD = 16


def stack_rows(rows, width=LANES):
    sub = lax.broadcasted_iota(jnp.int32, (SUB, width), 0)
    out = jnp.zeros((SUB, width), F32)
    for p, row in enumerate(rows):
        out = jnp.where(sub == p, row, out)
    return out


def local_kernel(
    sizes, shape, factors,
    u_ref, s_ref, bz_hbm, zmom_hbm, ytab_hbm, yw_hbm, xw_hbm, by_hbm, bx_hbm, zadd_hbm, xtab_ref,
    g_v, cz_ref, cy_ref, cx_ref, zadd_ref,
    bz_ref, zmom_ref, yw_ref, xw_ref, by_ref, bx_ref, tsem,
    u_v, sg_ref, ytab_ref, edge_v, xland, s_v, fh0, fl0, fh1, fl1, y0, y1, hy, mxf, mxu, mx, my, mz,
    zbuf, zpad, ybuf, xpair, xtot, xbuf, xback, eown, ebuf, qown, qbuf, rown, rbuf, town, tbuf, face,
    usem, ssem, hs, hr, zs, zr, ys, yr, ps, pr, xs, xr, bs, br, es, er, qs, qr, rs, rr, ts, tr,
):
    gx, gy, gz = lax.axis_index("gx"), lax.axis_index("gy"), lax.axis_index("gz")
    nx, ny, nz = sizes
    east, north, upward = shape
    tiles = upward // LANES
    steps = north // SUB
    chunks = east // PLANES
    pairs = chunks // 2
    blocks = east // LOAD
    rx, ry, _ = factors
    chips = nx // 2
    half = north // 2
    chip, core = gx // 2, lax.rem(gx, 2)
    mine = pl.ds(pl.multiple_of(core * half, half), half)
    theirs = pl.ds(pl.multiple_of((1 - core) * half, half), half)
    partner = at("gx", chip * 2 + 1 - core)

    def u_loads(b):
        rows = pl.ds(b * LOAD, LOAD)
        return [
            pltpu.make_async_copy(
                u_ref.at[rows, pl.ds(k * steps, steps), :], u_v.at[pl.ds(1 + b * LOAD, LOAD), :, k, :],
                usem.at[b, k])
            for k in range(SUB)
        ]

    def s_loads(b):
        rows = pl.ds(b * LOAD, LOAD)
        return [
            pltpu.make_async_copy(
                s_ref.at[rows, pl.ds(k * steps, steps), :], s_v.at[rows, :, k, :], ssem.at[b, k])
            for k in range(SUB)
        ]

    early = sorted({0, blocks - 1})
    for b in early + [b for b in range(blocks) if b not in early]:
        for copy in u_loads(b):
            copy.start()
    table_loads = [
        pltpu.make_async_copy(hbm.at[index], ref, tsem.at[n])
        for n, (hbm, index, ref) in enumerate((
            (bz_hbm, gz, bz_ref), (zmom_hbm, gz, zmom_ref), (ytab_hbm, gy, ytab_ref), (yw_hbm, gy, yw_ref),
            (xw_hbm, gx, xw_ref), (by_hbm, gy, by_ref), (bx_hbm, gx, bx_ref),
            (zadd_hbm, gz, zadd_ref)))
    ]
    for copy in table_loads:
        copy.start()

    def ring(axis, me, count):
        return [at(axis, lax.rem(me + o, count)) for o in range(1, count)]

    greet(ring("gx", gx, nx) + ring("gy", gy, ny) + ring("gz", gz, nz))

    xr_, xl_ = lax.rem(gx + 1, nx), lax.rem(gx + nx - 1, nx)
    yr_, yl_ = lax.rem(gy + 1, ny), lax.rem(gy + ny - 1, ny)
    halos = [
        remote(u_ref.at[:, north - 1, :], hy.at[0], hs.at[2], hr.at[2], at("gy", yr_)),
        remote(u_ref.at[:, 0, :], hy.at[1], hs.at[3], hr.at[3], at("gy", yl_)),
        remote(u_v.at[east], u_v.at[0], hs.at[0], hr.at[0], at("gx", xr_)),
        remote(u_v.at[1], u_v.at[east + 1], hs.at[1], hr.at[1], at("gx", xl_)),
    ]
    for copy in halos[:2]:
        copy.start()
    for b in early:
        for copy in u_loads(b):
            copy.wait()
    for copy in halos[2:]:
        copy.start()
    for b in range(blocks):
        for copy in s_loads(b):
            copy.start()

    sub = lax.broadcasted_iota(jnp.int32, (SUB, LANES), 0)

    def cols(l):
        return slice(l * LANES, (l + 1) * LANES)

    def rows_at(t):
        return slice(t * SUB, (t + 1) * SUB)

    mxu[...] = jnp.zeros_like(mxu)
    mxf[...] = jnp.zeros_like(mxf)
    zpad[...] = jnp.zeros_like(zpad)

    def weights(base):
        return [[xtab_ref[kind, gx * east + base + p] for p in range(PLANES)] for kind in range(2)]

    def pre(c, carry):
        block = c * PLANES // LOAD
        waits = lax.rem(c * PLANES, LOAD) == 0
        for b in early:
            waits = jnp.logical_and(waits, block != b)

        @pl.when(waits)
        def _():
            for copy in u_loads(block):
                copy.wait()

        base = c * PLANES
        w = weights(base)
        for l in range(tiles):
            for t in range(steps):
                acc = [mxu[kind, rows_at(t), cols(l)] for kind in range(2)]
                for p in range(PLANES):
                    own = u_v[base + p + 1, t, :, cols(l)]
                    for kind in range(2):
                        acc[kind] = acc[kind] + w[kind][p] * own
                for kind in range(2):
                    mxu[kind, rows_at(t), cols(l)] = acc[kind]
        return carry

    lax.fori_loop(0, chunks, pre, 0)

    for copy in halos:
        copy.wait()
    before = jnp.where(gx > 0, 1.0, 0.0).astype(F32)
    after = jnp.where(gx < nx - 1, 1.0, 0.0).astype(F32)
    south = jnp.where(gy > 0, 1.0, 0.0).astype(F32)
    nord = jnp.where(gy < ny - 1, 1.0, 0.0).astype(F32)
    u_v[0] = u_v[0] * before
    u_v[east + 1] = u_v[east + 1] * after

    for copy in table_loads:
        copy.wait()
    zmom = zmom_ref[...]
    halves = ((fh0, fl0), (fh1, fl1))

    def z_moments(source, k, c):
        flat = jnp.concatenate([f[k].reshape(PLANES * north, upward) for f in source], 1)
        mom = jnp.dot(flat, jnp.concatenate([zmom, zmom], 0), preferred_element_type=F32)
        across = [mom[p * north:(p + 1) * north].T for p in range(PLANES)]
        for kind in range(2):
            mz[kind, pl.ds(pl.multiple_of(c * PLANES, PLANES), PLANES), :] = stack_rows(
                [a[2 * kind:2 * kind + 1] + a[2 * kind + 1:2 * kind + 2] for a in across])

    def rhs(target, k, c):
        high_ref, low_ref = target
        base = pl.multiple_of(c * PLANES, PLANES)
        w = weights(base)
        for l in range(tiles):
            col = cols(l)
            edge = [hy[0, pl.ds(base, PLANES), col] * south, hy[1, pl.ds(base, PLANES), col] * nord]
            for t2 in range(0, steps, 2):
                acc = [[mxf[kind, rows_at(t2 + j), col] for j in range(2)] for kind in range(2)]
                column = [[u_v[base + p, t2 + j, :, col] for p in range(PLANES + 2)] for j in range(2)]
                for p in range(PLANES):
                    i = base + p
                    if t2 == 0:
                        below = pltpu.roll(u_v[i + 1, steps - 1, :, col], 1, 0)
                        below = jnp.where(sub == 0, edge[0][p:p + 1], below)
                    else:
                        below = u_v[i + 1, t2 - 1, :, col]
                    if t2 == steps - 2:
                        above = pltpu.roll(u_v[i + 1, 0, :, col], SUB - 1, 0)
                        above = jnp.where(sub == SUB - 1, edge[1][p:p + 1], above)
                    else:
                        above = u_v[i + 1, t2 + 2, :, col]
                    out = []
                    for j in range(2):
                        own = column[j][p + 1]
                        across = column[j][p] + column[j][p + 2]
                        along = (below + column[1][p + 1]) if j == 0 else (column[0][p + 1] + above)
                        if rx == ry:
                            spread = rx * ((across + along) + (2.0 / rx - 4.0) * own)
                        else:
                            spread = rx * across + ry * along + (2.0 - 2.0 * rx - 2.0 * ry) * own
                        f = s_v[i, t2 + j, :, col] + spread
                        for kind in range(2):
                            acc[kind][j] = acc[kind][j] + w[kind][p] * f
                        out.append(f)
                    pair = jnp.concatenate(out, 0)
                    high = pair.astype(BF16)
                    rows = slice(t2 * SUB, (t2 + 2) * SUB)
                    high_ref[k, p, rows, col] = high
                    low_ref[k, p, rows, col] = (pair - high.astype(F32)).astype(BF16)
                for kind in range(2):
                    for j in range(2):
                        mxf[kind, rows_at(t2 + j), col] = acc[kind][j]

    def rhs_pair(k, carry):
        waits = lax.rem(k * 2 * PLANES, LOAD) == 0

        @pl.when(waits)
        def _():
            for copy in s_loads(k * 2 * PLANES // LOAD):
                copy.wait()

        late = jnp.maximum(k - 1, 0)
        z_moments(halves[1], late, 2 * late + 1)
        rhs(halves[0], k, 2 * k)
        z_moments(halves[0], k, 2 * k)
        rhs(halves[1], k, 2 * k + 1)
        return carry

    lax.fori_loop(0, pairs, rhs_pair, 0)
    z_moments(halves[1], pairs - 1, chunks - 1)

    zcopies = [
        remote(mz.at[kind_to(gz, nz, o)], zbuf.at[o - 1], zs.at[o - 1], zr.at[o - 1],
               at("gz", lax.rem(gz + o, nz)))
        for o in range(1, nz)
    ]
    for copy in zcopies:
        copy.start()

    def solve_up(high, low):
        stack = jnp.concatenate([bz_ref[1], bz_ref[0], bz_ref[0]], 0)
        return jnp.dot(jnp.concatenate([high, low, high], 1), stack, preferred_element_type=F32)

    fold_h, fold_l = split(mxf[...].reshape(2 * north, upward))
    mx[...] = solve_up(fold_h, fold_l).reshape(2, north, upward) - 2.0 * mxu[...]

    pair = remote(mx.at[:, theirs, :], xpair, ps, pr, partner)
    pair.start()
    for kind in range(2):
        qown[kind] = dot(yw_ref[kind, 0], mx[0]) + dot(yw_ref[kind, 1], mx[1])
    qcopies = [
        remote(qown.at[kind_to(gy, ny, o)], qbuf.at[o - 1], qs.at[o - 1], qr.at[o - 1],
               at("gy", lax.rem(gy + o, ny)))
        for o in range(1, ny)
    ]
    for copy in qcopies:
        copy.start()
    xcopies = [
        remote(xtot.at[kind_to(chip, chips, o)], xbuf.at[o - 1], xs.at[o - 1], xr.at[o - 1],
               at("gx", lax.rem(chip + o, chips) * 2 + core))
        for o in range(1, chips)
    ]
    rcopies = [
        remote(rown.at[kind_to(gx, nx, o)], rbuf.at[o - 1], rs.at[o - 1], rr.at[o - 1],
               at("gx", lax.rem(gx + o, nx)))
        for o in range(1, nx)
    ]

    def send_chips():
        pair.wait()
        xtot[0] = mx[0, mine, :] + xpair[0]
        xtot[1] = mx[1, mine, :] + xpair[1]
        for copy in xcopies:
            copy.start()

    def send_edges():
        for copy in qcopies:
            copy.wait()
        qleft, qright = gather(gy, ny, qbuf)
        for kind in range(2):
            rown[kind] = stack_rows([qleft[kind:kind + 1], qright[kind:kind + 1]], upward)
        for copy in rcopies:
            copy.start()

    ecopies = [
        remote(eown.at[kind_to(gy, ny, o)], ebuf.at[o - 1], es.at[o - 1], er.at[o - 1],
               at("gy", lax.rem(gy + o, ny)))
        for o in range(1, ny)
    ]
    tcopies = [
        remote(town.at[kind_to(gx, nx, o)], tbuf.at[o - 1], ts.at[o - 1], tr.at[o - 1],
               at("gx", lax.rem(gx + o, nx)))
        for o in range(1, nx)
    ]

    def z_rows():
        for copy in zcopies:
            copy.wait()
        for m, value in enumerate(gather(gz, nz, zbuf)):
            zpad[m, 0:east] = value
        for kind in range(2):
            eown[kind] = dot(yw_ref[kind, 0], zpad[0], NT) + dot(yw_ref[kind, 1], zpad[1], NT)
        for copy in ecopies:
            copy.start()
        for m in range(2):
            face[m] = dot(zpad[m, 0:east], by_ref[...])

    def z_planes():
        for copy in ecopies:
            copy.wait()
        eleft, eright = gather(gy, ny, ebuf)
        value = [
            face[m] + (dot(eleft, yw_ref[1, m], TN) + dot(eright, yw_ref[0, m], TN))[0:east]
            for m in range(2)
        ]
        for kind in range(2):
            town[kind] = dot(xw_ref[kind, 0], value[0]) + dot(xw_ref[kind, 1], value[1])
        for copy in tcopies:
            copy.start()
        for m in range(2):
            face[m] = dot(bx_ref[...], value[m])

    parts = (max(chunks - 3, 1) * PLANES, east)
    ycopies = [
        [
            remote(my.at[kind_to(gy, ny, o), pl.ds(n * parts[0], parts[n] - n * parts[0])],
                   ybuf.at[o - 1, pl.ds(n * parts[0], parts[n] - n * parts[0])],
                   ys.at[n, o - 1], yr.at[n, o - 1], at("gy", lax.rem(gy + o, ny)))
            for o in range(1, ny)
        ]
        for n in range(2)
    ]

    def send_rows(n):
        for copy in ycopies[n]:
            copy.start()

    def multiply(source, k, target):
        high_ref, low_ref = source
        target[...] = solve_up(
            high_ref[k].reshape(PLANES * north, upward), low_ref[k].reshape(PLANES * north, upward))

    def finish(source, c):
        base = pl.multiple_of(c * PLANES, PLANES)
        for l in range(tiles):
            col = cols(l)
            sums = [[None] * PLANES for _ in range(2)]
            for t in range(steps):
                w = [ytab_ref[kind, rows_at(t)] for kind in range(2)]
                for p in range(PLANES):
                    i = base + p
                    own = u_v[i + 1, t, :, col]
                    g = source[p * north + t * SUB:p * north + (t + 1) * SUB, col] - 2.0 * own
                    g_v[i, t, :, col] = g
                    for kind in range(2):
                        term = w[kind] * g
                        sums[kind][p] = term if t == 0 else sums[kind][p] + term
            for kind in range(2):
                for p in range(PLANES):
                    sg_ref[kind, base + p, :, col] = sums[kind][p]
                my[kind, pl.ds(base, PLANES), col] = stack_rows(
                    [jnp.sum(sums[kind][p], 0, keepdims=True) for p in range(PLANES)])

    def solve_pair(k, carry):
        @pl.when(k == min(1, pairs - 1))
        def _():
            send_chips()

        @pl.when(k == max(pairs - 2, 0))
        def _():
            z_rows()

        @pl.when(k == pairs - 1)
        def _():
            send_rows(0)
            send_edges()

        multiply(halves[0], k, y0)
        finish(y1, jnp.maximum(2 * k - 1, 0))
        multiply(halves[1], k, y1)
        finish(y0, 2 * k)
        return carry

    lax.fori_loop(0, pairs, solve_pair, 0)
    finish(y1, chunks - 1)

    send_rows(1)
    z_planes()

    by = by_ref[...]
    edge_v[0] = jnp.zeros((north, upward), F32)
    edge_v[1] = dot(by, mx[1])

    def scan(value, backward):
        def shifted(x, d):
            if backward:
                return jnp.where(sub < SUB - d, pltpu.roll(x, SUB - d, 0), 0.0)
            return jnp.where(sub >= d, pltpu.roll(x, d, 0), 0.0)

        for d in (1, 2, 4):
            value = value + shifted(value, d)
        return shifted(value, 1)

    first = jnp.where(core == 0, 1.0, 0.0).astype(F32)
    second = 1.0 - first
    back = remote(xback, xland, bs, br, partner)

    def return_chips():
        for copy in xcopies:
            copy.wait()
        px, sx = gather(chip, chips, xbuf)
        xback[0] = px + first * mx[0, mine, :]
        xback[1] = sx + second * mx[1, mine, :]
        back.start()
        cx_ref[0, mine, :] = px + second * xpair[0]
        cx_ref[1, mine, :] = sx + first * xpair[1]

    def sweep(c, carry):
        @pl.when(c == min(2, chunks - 1))
        def _():
            return_chips()

        base = pl.multiple_of(c * PLANES, PLANES)
        wx = weights(base)
        for l in range(tiles):
            col = cols(l)
            low, high = [], []
            for p in range(PLANES):
                su, sv = sg_ref[0, base + p, :, col], sg_ref[1, base + p, :, col]
                low.append(scan(su, False))
                high.append(scan(sv, True) + sv)
            for t in range(steps):
                wu, wv = ytab_ref[0, rows_at(t)], ytab_ref[1, rows_at(t)]
                below, above = edge_v[0, rows_at(t), col], edge_v[1, rows_at(t), col]
                for p in range(PLANES):
                    i = base + p
                    g = g_v[i, t, :, col]
                    low[p] = low[p] + wu * g
                    high[p] = high[p] - wv * g
                    h = wv * low[p] + wu * high[p]
                    below = below + wx[0][p] * h
                    above = above - wx[1][p] * h
                    g_v[i, t, :, col] = u_v[i + 1, t, :, col] + (wx[1][p] * below + wx[0][p] * above)
                edge_v[0, rows_at(t), col] = below
                edge_v[1, rows_at(t), col] = above
        return carry

    lax.fori_loop(0, chunks, sweep, 0)

    back.wait()
    cx_ref[0, theirs, :] = xland[0]
    cx_ref[1, theirs, :] = xland[1]
    cx_ref[0] = dot(by, cx_ref[0])
    cx_ref[1] = dot(by, cx_ref[1])

    for copy in tcopies:
        copy.wait()
    tleft, tright = gather(gx, nx, tbuf)
    for m in range(2):
        value = face[m] + dot(xw_ref[1, m], tleft, TN) + dot(xw_ref[0, m], tright, TN)
        high = value.astype(BF16).astype(F32)
        cz_ref[:, 3 * m, :] = high
        cz_ref[:, 3 * m + 1, :] = (value - high).astype(BF16).astype(F32)
        cz_ref[:, 3 * m + 2, :] = high
        cz_ref[:, 6 + m, :] = jnp.zeros_like(value)

    for copy in rcopies:
        copy.wait()
    rleft, rright = gather(gx, nx, rbuf)
    fixed = [dot(xw_ref[1, m], rleft, TN) + dot(xw_ref[0, m], rright, TN) for m in range(2)]
    for n in range(2):
        for copy in ycopies[n]:
            copy.wait()
    for m, face_y in enumerate(gather(gy, ny, ybuf)):
        value = dot(bx_ref[...], face_y) + fixed[m]
        high = value.astype(BF16).astype(F32)
        cy_ref[:, 3 * m, :] = high
        cy_ref[:, 3 * m + 1, :] = high
        cy_ref[:, 3 * m + 2, :] = (value - high).astype(BF16).astype(F32)
        cy_ref[:, 6 + m, :] = jnp.zeros_like(value)


def local_pass(u, s, tables, sizes):
    east, north, upward = u.shape
    nx, ny, nz = sizes
    steps = north // SUB
    pairs = east // (2 * PLANES)
    blocks = east // LOAD
    chips = nx // 2
    half = north // 2
    vmem = pl.BlockSpec(memory_space=pltpu.VMEM)
    smem = pl.BlockSpec(memory_space=pltpu.SMEM)
    hbm = pl.BlockSpec(memory_space=pltpu.HBM)
    dma = pltpu.SemaphoreType.DMA

    def buf(*dims):
        return pltpu.VMEM(dims, F32)

    def halves():
        return pltpu.VMEM((pairs, PLANES, north, upward), BF16)

    names = ("bz", "zmom", "y", "yw", "xw", "by", "bx", "zadd")
    return pl.pallas_call(
        functools.partial(local_kernel, sizes, u.shape, tables["factors"]),
        name="local",
        out_shape=(
            buf(east, steps, SUB, upward),
            buf(east, SUB, north),
            buf(east, SUB, upward),
            buf(2, north, upward),
            pltpu.VMEM((SUB, upward), BF16),
        ),
        in_specs=[hbm, hbm] + [hbm] * len(names) + [smem],
        out_specs=(vmem,) * 5,
        scratch_shapes=[
            pltpu.VMEM((2, upward, upward), BF16), pltpu.VMEM((upward, LANES), BF16),
            buf(2, 2, SUB, north), buf(2, 2, SUB, east), buf(north, north), buf(east, east),
            dma((len(names),)),
            buf(east + 2, steps, SUB, upward),
            buf(2, east, SUB, upward),
            buf(2, north, LANES),
            buf(2, north, upward),
            buf(2, half, upward),
            buf(east, steps, SUB, upward),
            halves(), halves(), halves(), halves(),
            buf(PLANES * north, upward), buf(PLANES * north, upward),
            buf(2, east, upward),
            buf(2, north, upward), buf(2, north, upward), buf(2, north, upward),
            buf(2, east, upward), buf(2, east, north),
            buf(nz - 1, east, north), buf(2, LANES, north), buf(ny - 1, east, upward),
            buf(2, half, upward), buf(2, half, upward), buf(chips - 1, half, upward), buf(2, half, upward),
            buf(2, SUB, LANES), buf(ny - 1, SUB, LANES),
            buf(2, SUB, upward), buf(ny - 1, SUB, upward),
            buf(2, SUB, upward), buf(nx - 1, SUB, upward),
            buf(2, SUB, north), buf(nx - 1, SUB, north), buf(2, east, north),
            dma((blocks, SUB)), dma((blocks, SUB)),
            dma((4,)), dma((4,)),
            dma((nz - 1,)), dma((nz - 1,)),
            dma((2, ny - 1)), dma((2, ny - 1)),
            dma, dma,
            dma((chips - 1,)), dma((chips - 1,)),
            dma, dma,
            dma((ny - 1,)), dma((ny - 1,)),
            dma((ny - 1,)), dma((ny - 1,)),
            dma((nx - 1,)), dma((nx - 1,)),
            dma((nx - 1,)), dma((nx - 1,)),
        ],
        compiler_params=pltpu.CompilerParams(
            collective_id=0, has_side_effects=True, vmem_limit_bytes=LOCAL_VMEM),
    )(*[pltpu.with_memory_space_constraint(a, pltpu.HBM) for a in [u, s] + [tables[name] for name in names + ("x",)]])


LOCAL_VMEM = 44 * 2**20
FINAL_VMEM = 24 * 2**20


def final_kernel(
    shape,
    t_v, cz_ref, cy_ref, cx_ref, zadd_ref, yadd_ref, xtab_ref,
    o_ref,
    o_v, osem,
):
    gx, gy = lax.axis_index("gx"), lax.axis_index("gy")
    east, north, upward = shape
    tiles = upward // LANES
    steps = north // SUB
    chunks = east // PLANES

    def stores(c):
        rows = pl.ds(c * PLANES, PLANES)
        return [
            pltpu.make_async_copy(
                o_v.at[rows, :, k, :], o_ref.at[rows, pl.ds(k * steps, steps), :], osem.at[c, k])
            for k in range(SUB)
        ]

    zadd = zadd_ref[...].astype(F32)
    yadd = yadd_ref[gy]

    def step(c, carry):
        base = pl.multiple_of(c * PLANES, PLANES)
        wx = [[xtab_ref[kind, gx * east + base + p] for p in range(PLANES)] for kind in range(2)]
        add = []
        for p in range(PLANES):
            left = jnp.concatenate([cz_ref[base + p], yadd], 0).T.astype(BF16)
            right = jnp.concatenate([zadd, cy_ref[base + p]], 0).astype(BF16)
            add.append(jnp.dot(left, right, preferred_element_type=F32))
        for l in range(tiles):
            col = slice(l * LANES, (l + 1) * LANES)
            for t in range(steps):
                row = slice(t * SUB, (t + 1) * SUB)
                below, above = cx_ref[0, row, col], cx_ref[1, row, col]
                for p in range(PLANES):
                    o_v[base + p, t, :, col] = (t_v[base + p, t, :, col] + add[p][row, col]) + (
                        wx[1][p] * below + wx[0][p] * above)
        for copy in stores(c):
            copy.start()
        return carry

    lax.fori_loop(0, chunks, step, 0)
    for c in range(chunks):
        for copy in stores(c):
            copy.wait()


def final_pass(t, cz, cy, cx, zadd, tables, shape):
    east, north, upward = shape
    steps = north // SUB
    chunks = east // PLANES
    vmem = pl.BlockSpec(memory_space=pltpu.VMEM)
    smem = pl.BlockSpec(memory_space=pltpu.SMEM)
    return pl.pallas_call(
        functools.partial(final_kernel, shape),
        name="final",
        out_shape=jax.ShapeDtypeStruct(shape, F32),
        in_specs=[vmem] * 6 + [smem],
        out_specs=pl.BlockSpec(memory_space=pl.ANY),
        scratch_shapes=[
            pltpu.VMEM((east, steps, SUB, upward), F32),
            pltpu.SemaphoreType.DMA((chunks, SUB)),
        ],
        compiler_params=pltpu.CompilerParams(vmem_limit_bytes=FINAL_VMEM),
    )(t, cz, cy, cx, zadd, tables["yadd"], tables["x"])


def local(sizes, u, s):
    tables = make_tables(u.shape, sizes)
    return final_pass(*local_pass(u, s, tables, sizes), tables, u.shape)


def solution(mesh):
    sizes = tuple(mesh.shape[name] for name in ("gx", "gy", "gz"))
    spec = P("gx", "gy", "gz")
    return jax.shard_map(
        functools.partial(local, sizes), mesh=mesh, in_specs=(spec, spec), out_specs=spec, check_vma=False
    )
```
